32 devices in a mesh: parts: 2 (over x), ctx: 16 (over z, y, core).
Axes of the slice: x: 2, y: 2, z: 4, core: 2. Of those that a mesh axis runs over, the one named last changes fastest.
Arguments:
- queries: bfloat16 [8192, 2048], P(('parts', 'ctx')), parts along dimension 0, may hold values from -6 to 6
- key_vectors: bfloat16 [8192, 2048], P(('parts', 'ctx')), parts along dimension 0, may hold values from -6 to 6
- value_vectors: bfloat16 [8192, 2048], P(('parts', 'ctx')), parts along dimension 0, may hold values from -6 to 6
- out_grad: bfloat16 [8192, 2048], P(('parts', 'ctx')), parts along dimension 0, may hold values from -6 to 6
- norm_gain: float32 [2048], replicated, may hold values from 0.5 to 1.5
- doc_bounds: int32 [2, 64], P(None, ('parts', 'ctx')), parts along dimension 1, may hold values from 0 to 31, as said below
Outputs:
- query_grad: bfloat16 [8192, 2048], P(('parts', 'ctx')), parts along dimension 0
- key_grad: bfloat16 [8192, 2048], P(('parts', 'ctx')), parts along dimension 0
- value_grad: bfloat16 [8192, 2048], P(('parts', 'ctx')), parts along dimension 0
- gain_grad: float32 [4096], P('parts'), parts along dimension 0
The draws below stay inside these ranges and needn't reach their ends.
There are 2 independent parts, one for each index of `parts`. The reference program is written for one: setup_inputs(seed, part) draws one part's arguments, and reference() takes and returns one part's arrays. A program takes and returns all parts, laid end to end along the dimension named above; an argument that names none is the same for every part. Nothing has to cross between parts.
Inputs may be any that keep to these rules, and one draw needn't show every extreme that they name: doc_bounds[0, b] and doc_bounds[1, b] are the first and last block of the document that holds block b; documents are runs of whole blocks of 128 tokens covering the sequence in order, and block 0 starts one.
All inputs are finite; a program needn't handle non-finite values.
Results may differ from the reference program's by a relative error of at most 0.011.
Values sent between devices are 32-bit elements; how exact they have to be, the bound alone decides.
No kernel may reach another device: no remote copies, remote signals or barrier semaphores. Data moves between devices by JAX's collectives and lax.ppermute only.
A program may use at most 64 MiB of HBM per device.

```python
import math
import jax
import jax.numpy as jnp
from jax import lax

E = 128
H = 16
BLK = 128
BLK_DEV = 2
TOK_DEV = 256
TOKENS = 4096
NBLOCKS = 32
N_CTX = 16


def draw_doc_bounds(key, part):
    picks = jax.random.randint(key, (NBLOCKS,), 0, NBLOCKS)
    places = jnp.arange(NBLOCKS, dtype=jnp.int32)
    starts = (picks < 4) | (places == 0)
    first_of = lax.cummax(jnp.where(starts, places, 0), axis=0)
    nexts = jnp.where(starts, places, NBLOCKS)
    shifted = jnp.concatenate([nexts[1:], jnp.full((1,), NBLOCKS, jnp.int32)])
    last_of = lax.cummin(shifted, axis=0, reverse=True) - 1
    return jnp.stack([first_of, last_of]).astype(jnp.int32)


def block_scale(rng, shape, split, least, high):
    gain, own = 1.0, jax.random.fold_in(rng, 6)
    for position, shards_of in split:
        steps = jnp.exp(jax.random.uniform(jax.random.fold_in(own, position), (shards_of,), jnp.float32, least / len(split), high / len(split)))
        gain = gain * jnp.repeat(steps, shape[position] // shards_of).reshape([-1 if axis == position else 1 for axis in range(len(shape))])
    return gain


def centred(key, extent, spread, limit, split=(), kind=jnp.bfloat16):
    level = block_scale(key, extent, split, -0.22, 0.18) if split else 1.0
    result = jax.random.normal(key, extent, jnp.float32) * spread * level
    return jnp.minimum(jnp.maximum(result, -limit), limit).astype(kind)


def setup_inputs(seed: int = 0, part: int = 0) -> dict:
    key_of = jax.random.split(jax.random.key(seed), 7)
    part_keys = jax.random.split(jax.random.fold_in(key_of[6], part), 7)
    return {
        "queries": centred(part_keys[0], (TOKENS, H * E), 1.0, 6.0, ((0, 16),)),
        "key_vectors": centred(part_keys[1], (TOKENS, H * E), 1.0, 6.0, ((0, 16),)),
        "value_vectors": centred(part_keys[2], (TOKENS, H * E), 1.0, 6.0, ((0, 16),)),
        "out_grad": centred(part_keys[3], (TOKENS, H * E), 1.0, 6.0, ((0, 16),)),
        "norm_gain": jnp.clip(jax.random.uniform(key_of[4], (H * E,), jnp.float32, 0.5, 1.5), 0.5, 1.5),
        "doc_bounds": draw_doc_bounds(jax.random.fold_in(jax.random.fold_in(key_of[6], part), 71), part),
    }


epsilon = 1e-06

def segment_flags(first_row, last_row, seg_index):
    dev_first = seg_index * BLK_DEV
    doc_first = jnp.repeat(first_row, BLK)
    doc_last = jnp.repeat(last_row, BLK)
    positions = jnp.arange(TOK_DEV, dtype=jnp.int32)
    causal_mask = (doc_first[:, None] == doc_first[None, :]) & (positions[None, :] <= positions[:, None])
    use_carry = (doc_first < dev_first)[:, None, None]
    tail_rows = (doc_last >= dev_first + BLK_DEV - 1)[:, None, None]
    reset_flag = (first_row[BLK_DEV - 1] >= dev_first).astype(jnp.float32)
    return (causal_mask, use_carry, tail_rows, reset_flag)

def masked_scores(left, right, causal_mask):
    raw = jnp.einsum('ihe,jhe->hij', left.astype(jnp.float32), right.astype(jnp.float32))
    return jnp.where(causal_mask[None], raw, 0.0).astype(jnp.bfloat16)

def reference(queries, key_vectors, value_vectors, out_grad, norm_gain, doc_bounds):
    shape_four = (N_CTX, TOK_DEV, H, E)
    query_all = queries.reshape(shape_four)
    key_all = key_vectors.reshape(shape_four)
    value_all = value_vectors.reshape(shape_four)
    grad_all = out_grad.reshape(shape_four).astype(jnp.float32)
    first_all = doc_bounds[0].reshape(N_CTX, BLK_DEV).astype(jnp.int32)
    last_all = doc_bounds[1].reshape(N_CTX, BLK_DEV).astype(jnp.int32)
    seg_ids = jnp.arange(N_CTX, dtype=jnp.int32)
    gain_heads = norm_gain.reshape(H, E)

    def forward_step(carry, inputs):
        query_seg, key_seg, value_seg, first_row, last_row, seg_index = inputs
        causal_mask, use_carry, tail_rows, reset_flag = segment_flags(first_row, last_row, seg_index)
        key_tail = jnp.where(tail_rows, key_seg, jnp.zeros_like(key_seg))
        state_part = jnp.einsum('jhe,jhf->hef', key_tail.astype(jnp.float32), value_seg.astype(jnp.float32))
        scores_b = masked_scores(query_seg, key_seg, causal_mask)
        local_out = jnp.einsum('hij,jhe->ihe', scores_b.astype(jnp.float32), value_seg.astype(jnp.float32))
        carried_b = carry.astype(jnp.bfloat16)
        from_carry = jnp.einsum('ihe,hef->ihf', query_seg.astype(jnp.float32), carried_b.astype(jnp.float32))
        attended = local_out + jnp.where(use_carry, from_carry, 0.0)
        return (state_part + (1.0 - reset_flag) * carry, (attended, carry))
    _, (attended, carried) = lax.scan(forward_step, jnp.zeros((H, E, E), jnp.float32), (query_all, key_all, value_all, first_all, last_all, seg_ids))
    root = jnp.sqrt(lax.optimization_barrier(jnp.mean(attended * attended, axis=-1, keepdims=True)) + epsilon)
    normed = attended / root
    gain_grad = lax.optimization_barrier(jnp.sum(grad_all * normed, axis=(0, 1))).reshape(H * E) / math.sqrt(TOKENS)
    dnormed = grad_all * gain_heads
    d_att = ((dnormed - normed * lax.optimization_barrier(jnp.mean(dnormed * normed, axis=-1, keepdims=True))) / root).astype(jnp.bfloat16)

    def backward_step(carry, inputs):
        query_seg, key_seg, value_seg, datt_seg, carried_seg, first_row, last_row, seg_index = inputs
        causal_mask, use_carry, tail_rows, reset_flag = segment_flags(first_row, last_row, seg_index)
        query_used = jnp.where(use_carry, query_seg, jnp.zeros_like(query_seg))
        grad_part = jnp.einsum('ihe,ihf->hef', query_used.astype(jnp.float32), datt_seg.astype(jnp.float32))
        later_b = carry.astype(jnp.bfloat16).astype(jnp.float32)
        carried_b = carried_seg.astype(jnp.bfloat16).astype(jnp.float32)
        scores_b = masked_scores(query_seg, key_seg, causal_mask).astype(jnp.float32)
        dscores_b = masked_scores(datt_seg, value_seg, causal_mask).astype(jnp.float32)
        query_f = query_seg.astype(jnp.float32)
        key_f = key_seg.astype(jnp.float32)
        value_f = value_seg.astype(jnp.float32)
        datt_f = datt_seg.astype(jnp.float32)
        query_grad = jnp.einsum('hij,jhe->ihe', dscores_b, key_f) + jnp.where(use_carry, jnp.einsum('ihf,hef->ihe', datt_f, carried_b), 0.0)
        key_grad = jnp.einsum('hij,ihe->jhe', dscores_b, query_f) + jnp.where(tail_rows, jnp.einsum('jhf,hef->jhe', value_f, later_b), 0.0)
        value_grad = jnp.einsum('hij,ihe->jhe', scores_b, datt_f) + jnp.where(tail_rows, jnp.einsum('jhe,hef->jhf', key_f, later_b), 0.0)
        outs = (query_grad.astype(jnp.bfloat16), key_grad.astype(jnp.bfloat16), value_grad.astype(jnp.bfloat16))
        return (grad_part + (1.0 - reset_flag) * carry, outs)
    _, (query_grad, key_grad, value_grad) = lax.scan(backward_step, jnp.zeros((H, E, E), jnp.float32), (query_all, key_all, value_all, d_att, carried, first_all, last_all, seg_ids), reverse=True)
    return (query_grad.reshape(TOKENS, H * E), key_grad.reshape(TOKENS, H * E), value_grad.reshape(TOKENS, H * E), gain_grad)
```

```python
import functools
import math

import jax
import jax.numpy as jnp
from jax import lax
from jax.experimental import pallas as pl
from jax.experimental.pallas import tpu as pltpu
from jax.sharding import PartitionSpec as P

E = 128
PAIR = 2 * E
FLAG = 8
EPS = 1e-06
F32 = jnp.float32
BF16 = jnp.bfloat16


def dot(a, b, a_dim, b_dim):
    return lax.dot_general(a, b, (((a_dim,), (b_dim,)), ((), ())), preferred_element_type=F32)


def row_values(values, rows, block_len):
    position = lax.broadcasted_iota(jnp.int32, (rows, E), 0)
    result = jnp.full((rows, E), values[0], values[0].dtype)
    for block in range(1, len(values)):
        result = jnp.where(position >= block * block_len, values[block], result)
    return result


def flags(bounds, block_count):
    first = lax.axis_index("ctx") * block_count
    use = [(bounds[0, b] < first).astype(F32) for b in range(block_count)]
    tail = [(bounds[1, b] >= first + block_count - 1).astype(F32) for b in range(block_count)]
    reset = (bounds[0, block_count - 1] >= first).astype(F32)
    return use, tail, reset


def place(step, pairs):
    y_bit = (lax.axis_index("ctx") // 2) % 2
    slot = ((step % 2) ^ y_bit) * (pairs // 2) + step // 2
    return pl.ds(pl.multiple_of(slot * E, E), E)


def state_kernel(bounds, k_ref, v_ref, keep_ref, send_ref, tail_ref, *, block_count, pairs):
    step = pl.program_id(0)
    rows = k_ref.shape[0]
    core = lax.axis_index("ctx") % 2

    @pl.when(step == 0)
    def _():
        _, tail, reset = flags(bounds, block_count)
        tail_ref[...] = row_values(tail, rows, rows // block_count).astype(BF16)
        send_ref[pairs * E :, :] = jnp.full((FLAG, E), reset, F32)

    tail_rows = tail_ref[...]
    states = []
    for half in range(2):
        columns = slice(half * E, (half + 1) * E)
        states.append(dot(k_ref[:, columns] * tail_rows, v_ref[:, columns], 0, 0))
    where = place(step, pairs)
    keep_ref[where, :] = jnp.where(core == 0, states[0], states[1])
    send_ref[where, :] = jnp.where(core == 0, states[1], states[0])


def main_kernel(
    bounds, q_ref, k_ref, v_ref, g_ref, gain_ref, kept_ref, got_ref,
    qg_ref, kp_ref, vp_ref, keep_ref, send_ref, mask_ref, use_ref,
    *, block_count, pairs,
):
    step = pl.program_id(0)
    rows = q_ref.shape[0]
    core = lax.axis_index("ctx") % 2

    @pl.when(step == 0)
    def _():
        use, _, reset = flags(bounds, block_count)
        block_len = rows // block_count
        use_ref[...] = row_values(use, rows, block_len).astype(BF16)
        row = lax.broadcasted_iota(jnp.int32, (rows, rows), 0)
        column = lax.broadcasted_iota(jnp.int32, (rows, rows), 1)
        row_doc = jnp.full((rows, rows), bounds[0, 0], jnp.int32)
        column_doc = row_doc
        for block in range(1, block_count):
            row_doc = jnp.where(row >= block * block_len, bounds[0, block], row_doc)
            column_doc = jnp.where(column >= block * block_len, bounds[0, block], column_doc)
        seen = (row_doc == column_doc) & (column <= row)
        mask_ref[...] = jnp.where(seen, 1.0, 0.0).astype(BF16)
        send_ref[pairs * E : pairs * E + FLAG, :] = jnp.full((FLAG, E), reset, F32)

    where = place(step, pairs)
    kept, got = kept_ref[where, :], got_ref[where, :]
    carries = (
        jnp.where(core == 0, kept, got).astype(BF16),
        jnp.where(core == 0, got, kept).astype(BF16),
    )
    use_rows = use_ref[...]
    states = []
    for half in range(2):
        columns = slice(half * E, (half + 1) * E)
        query, key, value = q_ref[:, columns], k_ref[:, columns], v_ref[:, columns]
        carry = carries[half]
        query_used = query * use_rows
        scores = dot(query, key, 1, 1).astype(BF16) * mask_ref[...]
        attended = dot(scores, value, 1, 0) + dot(query_used, carry, 1, 0)
        inverse = 1.0 / jnp.sqrt(jnp.mean(attended * attended, axis=1, keepdims=True) + EPS)
        normed = attended * inverse
        grad = g_ref[:, columns].astype(F32)
        gained = grad * normed
        send_ref[pl.ds(pairs * E + FLAG + 2 * step + half, 1), :] = jnp.sum(gained, axis=0, keepdims=True)
        gain = gain_ref[:, columns]
        centre = jnp.mean(gained * gain, axis=1, keepdims=True)
        d_att = ((grad * gain - normed * centre) * inverse).astype(BF16)
        states.append(dot(query_used, d_att, 0, 0))
        dscores = dot(d_att, value, 1, 1).astype(BF16) * mask_ref[...]
        qg_ref[:, columns] = (dot(dscores, key, 1, 0) + dot(d_att * use_rows, carry, 1, 1)).astype(BF16)
        kp_ref[:, columns] = dot(dscores, query, 0, 0)
        vp_ref[:, columns] = dot(scores, d_att, 0, 0)
    keep_ref[where, :] = jnp.where(core == 0, states[0], states[1])
    send_ref[where, :] = jnp.where(core == 0, states[1], states[0])


def final_kernel(bounds, k_ref, v_ref, kp_ref, vp_ref, kept_ref, got_ref, kg_ref, vg_ref, tail_ref, *, block_count, pairs):
    step = pl.program_id(0)
    rows = k_ref.shape[0]
    core = lax.axis_index("ctx") % 2

    @pl.when(step == 0)
    def _():
        _, tail, _ = flags(bounds, block_count)
        tail_ref[...] = row_values(tail, rows, rows // block_count).astype(BF16)

    where = place(step, pairs)
    kept, got = kept_ref[where, :], got_ref[where, :]
    laters = (
        jnp.where(core == 0, kept, got).astype(BF16),
        jnp.where(core == 0, got, kept).astype(BF16),
    )
    tail_rows = tail_ref[...]
    for half in range(2):
        columns = slice(half * E, (half + 1) * E)
        later = laters[half]
        kg_ref[:, columns] = (kp_ref[:, columns] + dot(v_ref[:, columns] * tail_rows, later, 1, 1)).astype(BF16)
        vg_ref[:, columns] = (vp_ref[:, columns] + dot(k_ref[:, columns] * tail_rows, later, 1, 0)).astype(BF16)


def swap(block, distance):
    count = lax.axis_size("ctx")
    return lax.ppermute(block, "ctx", [(i, i ^ distance) for i in range(count)])


def scan(keep, send, backward):
    count = lax.axis_size("ctx")
    me = lax.axis_index("ctx")
    rows = keep.shape[0]
    half = rows // 2

    def last(distance):
        return ((me // distance) % 2 == 1) != backward

    got = swap(send, 1)
    flag, got_flag = send[rows : rows + 1], got[rows : rows + 1]
    extra = send[rows + FLAG :] + got[rows + FLAG :]
    second = last(1)
    first_core = jnp.where(second, got[:rows], keep)
    core_flag = jnp.where(second, got_flag, flag)
    late, late_flag = jnp.where(second, keep, got[:rows]), jnp.where(second, flag, got_flag)
    total = late + (1.0 - late_flag) * first_core
    flag = jnp.maximum(flag, got_flag)

    def packed(block, flag, extra):
        return jnp.concatenate([block, jnp.broadcast_to(flag, (FLAG, E)), extra])

    send = packed(total[half:], flag, extra)
    keep = total[:half]
    got = swap(send, 2)
    got_flag = got[half : half + 1]
    extra = extra + got[half + FLAG :]
    second = last(2)
    first_chip = jnp.where(second, got[:half], keep)
    chip_flag = jnp.where(second, got_flag, flag)
    late, late_flag = jnp.where(second, keep, got[:half]), jnp.where(second, flag, got_flag)
    total = late + (1.0 - late_flag) * first_chip
    flag = jnp.maximum(flag, got_flag)

    before, before_flag = jnp.zeros_like(total), jnp.zeros_like(flag)
    distance = 4
    while distance < count:
        got = swap(packed(total, flag, extra), distance)
        got_total, got_flag = got[:half], got[half : half + 1]
        extra = extra + got[half + FLAG :]
        second = last(distance)
        before = jnp.where(second, before + (1.0 - before_flag) * got_total, before)
        before_flag = jnp.where(second, jnp.maximum(before_flag, got_flag), before_flag)
        total = jnp.where(
            second, total + (1.0 - flag) * got_total, got_total + (1.0 - got_flag) * total
        )
        flag = jnp.maximum(flag, got_flag)
        distance *= 2

    after = first_chip + (1.0 - chip_flag) * before
    second = last(2)
    mine, theirs = jnp.where(second, after, before), jnp.where(second, before, after)
    before = jnp.concatenate([mine, swap(theirs, 2)])
    after = first_core + (1.0 - core_flag) * before
    second = last(1)
    mine, theirs = jnp.where(second, after, before), jnp.where(second, before, after)
    return mine, swap(theirs, 1), extra


def shards(queries, key_vectors, value_vectors, out_grad, norm_gain, doc_bounds):
    tokens, width = queries.shape
    block_count = doc_bounds.shape[1]
    pairs = width // PAIR
    rows = pairs * E
    sizes = dict(block_count=block_count, pairs=pairs)
    columns = pl.BlockSpec((tokens, PAIR), lambda j, *_: (0, j))
    whole = lambda count: pl.BlockSpec((count, E), lambda j, *_: (0, 0))
    params = pltpu.CompilerParams(
        dimension_semantics=("arbitrary",), vmem_limit_bytes=48 * 1024 * 1024
    )

    def call(kernel, in_specs, out_specs, out_shape, scratch):
        return pl.pallas_call(
            functools.partial(kernel, **sizes),
            grid_spec=pltpu.PrefetchScalarGridSpec(
                num_scalar_prefetch=1,
                grid=(pairs,),
                in_specs=in_specs,
                out_specs=out_specs,
                scratch_shapes=scratch,
            ),
            out_shape=out_shape,
            compiler_params=params,
        )

    keep, send = call(
        state_kernel,
        [columns, columns],
        [whole(rows), whole(rows + FLAG)],
        [jax.ShapeDtypeStruct((rows, E), F32), jax.ShapeDtypeStruct((rows + FLAG, E), F32)],
        [pltpu.VMEM((tokens, E), BF16)],
    )(doc_bounds, key_vectors, value_vectors)
    kept, got, _ = scan(keep, send, False)
    extra = rows + FLAG + 2 * pairs
    query_grad, key_part, value_part, keep, send = call(
        main_kernel,
        [columns] * 4 + [pl.BlockSpec((1, PAIR), lambda j, *_: (0, j))] + [whole(rows)] * 2,
        [columns] * 3 + [whole(rows), whole(extra)],
        [
            jax.ShapeDtypeStruct((tokens, width), BF16),
            jax.ShapeDtypeStruct((tokens, width), F32),
            jax.ShapeDtypeStruct((tokens, width), F32),
            jax.ShapeDtypeStruct((rows, E), F32),
            jax.ShapeDtypeStruct((extra, E), F32),
        ],
        [pltpu.VMEM((tokens, tokens), BF16), pltpu.VMEM((tokens, E), BF16)],
    )(doc_bounds, queries, key_vectors, value_vectors, out_grad, norm_gain.reshape(1, width), kept, got)
    kept, got, gain = scan(keep, send, True)
    key_grad, value_grad = call(
        final_kernel,
        [columns] * 4 + [whole(rows)] * 2,
        [columns] * 2,
        [jax.ShapeDtypeStruct((tokens, width), BF16)] * 2,
        [pltpu.VMEM((tokens, E), BF16)],
    )(doc_bounds, key_vectors, value_vectors, key_part, value_part, kept, got)
    gain_grad = gain.reshape(width) / math.sqrt(tokens * lax.axis_size("ctx"))
    return query_grad, key_grad, value_grad, gain_grad


def solution(mesh):
    tokens = P(("parts", "ctx"), None)
    return jax.shard_map(
        shards,
        mesh=mesh,
        in_specs=(tokens, tokens, tokens, tokens, P(), P(None, ("parts", "ctx"))),
        out_specs=(tokens, tokens, tokens, P("parts")),
        check_vma=False,
    )
```

```python
import functools
import math

import jax
import jax.numpy as jnp
from jax import lax
from jax.experimental import pallas as pl
from jax.experimental.pallas import tpu as pltpu
from jax.sharding import PartitionSpec as P

E = 128
PAIR = 2 * E
FLAG = 8
EPS = 1e-06
VMEM_LIMIT = 8 * 1024 * 1024
F32 = jnp.float32
BF16 = jnp.bfloat16
VMEM = pl.BlockSpec(memory_space=pltpu.VMEM)
ANY = pl.BlockSpec(memory_space=pl.ANY)


def dot(a, b, a_dim, b_dim):
    return lax.dot_general(a, b, (((a_dim,), (b_dim,)), ((), ())), preferred_element_type=F32)


def head(h):
    return slice(h * E, (h + 1) * E)


def both(pair):
    return slice(pair * PAIR, (pair + 1) * PAIR)


def place(pair, pairs):
    y_bit = (lax.axis_index("ctx") // 2) % 2
    slot = ((pair % 2) ^ y_bit) * (pairs // 2) + pair // 2
    return pl.ds(pl.multiple_of(slot * E, E), E)


def put_states(states, pair, pairs, keep_ref, send_ref):
    where = place(pair, pairs)
    core = lax.axis_index("ctx") % 2
    keep_ref[where, :] = jnp.where(core == 0, states[0], states[1])
    send_ref[where, :] = jnp.where(core == 0, states[1], states[0])


def get_states(pair, pairs, kept_ref, got_ref):
    where = place(pair, pairs)
    core = lax.axis_index("ctx") % 2
    kept, got = kept_ref[where, :], got_ref[where, :]
    return (
        jnp.where(core == 0, kept, got).astype(BF16),
        jnp.where(core == 0, got, kept).astype(BF16),
    )


def fetch(group, sources, targets, sems):
    width = targets[0].shape[1]
    copies = []
    for pair in range(width // PAIR):
        copies.append([])
        for i, (source, target) in enumerate(zip(sources, targets)):
            copy = pltpu.make_async_copy(
                source.at[:, pl.ds(group * width + pair * PAIR, PAIR)],
                target.at[:, both(pair)],
                sems.at[pair, i],
            )
            copy.start()
            copies[-1].append(copy)
    return copies


def row_values(values, rows, dtype):
    position = lax.broadcasted_iota(jnp.int32, (rows, E), 0)
    result = jnp.full((rows, E), values[0])
    for block in range(1, len(values)):
        result = jnp.where(position >= block * (rows // len(values)), values[block], result)
    return result.astype(dtype)


def states_of(k_ref, v_ref, tail_ref, copies, keep_ref, send_ref):
    pairs = len(copies)
    tail = tail_ref[...]
    for pair in range(pairs):
        for copy in copies[pair]:
            copy.wait()
        states = [
            dot(k_ref[:, head(h)] * tail, v_ref[:, head(h)], 0, 0) for h in (2 * pair, 2 * pair + 1)
        ]
        put_states(states, pair, pairs, keep_ref, send_ref)


def first_state_kernel(
    bounds_hbm, k_hbm, v_hbm,
    keep_ref, send_ref, k_ref, v_ref, start_ref, end_ref, use_ref, tail_ref, flag_ref, bits_ref,
    bounds, sems, bounds_sem, *, group,
):
    bounds_copy = pltpu.make_async_copy(bounds_hbm, bounds, bounds_sem)
    bounds_copy.start()
    copies = fetch(group, (k_hbm, v_hbm), (k_ref, v_ref), sems)
    rows, width = k_ref.shape
    count = bounds.shape[1]
    block_len = rows // count
    me = lax.axis_index("ctx")
    first = me * count
    for bit in range(bits_ref.shape[0] // FLAG):
        value = jnp.full((FLAG, E), (me // 2**bit) % 2)
        bits_ref[bit * FLAG : (bit + 1) * FLAG, :] = value.astype(F32)
    bounds_copy.wait()
    opens = [bounds[0, b] for b in range(count)]
    closes = [bounds[1, b] for b in range(count)]
    flag = jnp.full((FLAG, E), (opens[-1] >= first).astype(F32))
    flag_ref[...] = flag
    send_ref[width // 2 :, :] = flag
    use_ref[...] = row_values([(x < first).astype(F32) for x in opens], rows, BF16)
    tail_ref[...] = row_values([(x >= first + count - 1).astype(F32) for x in closes], rows, BF16)
    start_ref[...] = row_values([(x - first) * block_len for x in opens], rows, jnp.int32)
    end_ref[...] = row_values([(x - first + 1) * block_len for x in closes], rows, jnp.int32)
    states_of(k_ref, v_ref, tail_ref, copies, keep_ref, send_ref)


def state_kernel(
    k_hbm, v_hbm, tail_ref, flag_ref, keep_ref, send_ref, k_ref, v_ref, sems, *, group
):
    copies = fetch(group, (k_hbm, v_hbm), (k_ref, v_ref), sems)
    send_ref[k_ref.shape[1] // 2 :, :] = flag_ref[...]
    states_of(k_ref, v_ref, tail_ref, copies, keep_ref, send_ref)


def sight(bound_ref, turned):
    rows = bound_ref.shape[0]
    row = lax.broadcasted_iota(jnp.int32, (rows, E), 0)
    parts = []
    for c in range(rows // E):
        column = lax.broadcasted_iota(jnp.int32, (rows, E), 1) + c * E
        if turned:
            seen = (column >= row) & (column < bound_ref[...])
        else:
            seen = (column <= row) & (column >= bound_ref[...])
        parts.append(jnp.where(seen, 1.0, 0.0).astype(BF16))
    return jnp.concatenate(parts, axis=1)


def local_kernel(
    q_hbm, g_hbm, gain_hbm, k_ref, v_ref, start_ref, _,
    out_ref, q_ref, g_ref, gain_ref, sems, gain_sem, *, group,
):
    width = k_ref.shape[1]
    copies = fetch(group, (q_hbm, g_hbm), (q_ref, g_ref), sems)
    gain_copy = pltpu.make_async_copy(
        gain_hbm.at[:, pl.ds(group * width, width)], gain_ref, gain_sem
    )
    gain_copy.start()
    mask = sight(start_ref, False)
    for pair in range(width // PAIR):
        copies[pair][0].wait()
        for h in (2 * pair, 2 * pair + 1):
            scores = dot(q_ref[:, head(h)], k_ref[:, head(h)], 1, 1).astype(BF16) * mask
            out_ref[:, head(h)] = dot(scores, v_ref[:, head(h)], 1, 0)
    for pair in range(width // PAIR):
        copies[pair][1].wait()
    gain_copy.wait()


def middle_kernel(
    q_ref, g_ref, gain_ref, local_ref, kept_ref, got_ref, use_ref, flag_ref,
    d_ref, keep_ref, send_ref,
):
    pairs = q_ref.shape[1] // PAIR
    use = use_ref[...]
    send_ref[pairs * E : pairs * E + FLAG, :] = flag_ref[...]
    for pair in range(pairs):
        states = []
        for h, carry in zip((2 * pair, 2 * pair + 1), get_states(pair, pairs, kept_ref, got_ref)):
            used = q_ref[:, head(h)] * use
            attended = local_ref[:, head(h)] + dot(used, carry, 1, 0)
            inverse = lax.rsqrt(jnp.mean(attended * attended, axis=1, keepdims=True) + EPS)
            normed = attended * inverse
            grad = g_ref[:, head(h)].astype(F32)
            gained = grad * normed
            row = pairs * E + FLAG + h
            send_ref[row : row + 1, :] = jnp.sum(gained, axis=0, keepdims=True)
            gain = gain_ref[:, head(h)]
            centre = jnp.mean(gained * gain, axis=1, keepdims=True)
            d_att = ((grad * gain - normed * centre) * inverse).astype(BF16)
            d_ref[:, head(h)] = d_att
            states.append(dot(used, d_att, 0, 0))
        put_states(states, pair, pairs, keep_ref, send_ref)


def spread_kernel(
    q_ref, k_ref, v_ref, d_ref, kept_ref, got_ref, use_ref, start_ref, end_ref, *rest, group
):
    qg_hbm, kp_ref, vp_ref, qg_ref, sems = rest[-5:]
    width = q_ref.shape[1]
    pairs = width // PAIR
    use = use_ref[...]
    mask = sight(start_ref, False)
    turned_mask = sight(end_ref, True)
    copies = []
    for pair in range(pairs):
        for h, carry in zip((2 * pair, 2 * pair + 1), get_states(pair, pairs, kept_ref, got_ref)):
            c = head(h)
            query, key, value, d_att = q_ref[:, c], k_ref[:, c], v_ref[:, c], d_ref[:, c]
            dscores = dot(d_att, value, 1, 1).astype(BF16) * mask
            from_carry = dot(d_att * use, carry, 1, 1)
            qg_ref[:, c] = (dot(dscores, key, 1, 0) + from_carry).astype(BF16)
            turned = dot(value, d_att, 1, 1).astype(BF16) * turned_mask
            kp_ref[:, c] = dot(turned, query, 1, 0)
            turned = dot(key, query, 1, 1).astype(BF16) * turned_mask
            vp_ref[:, c] = dot(turned, d_att, 1, 0)
        copy = pltpu.make_async_copy(
            qg_ref.at[:, both(pair)],
            qg_hbm.at[:, pl.ds(group * width + pair * PAIR, PAIR)],
            sems.at[pair],
        )
        copy.start()
        copies.append(copy)
    for copy in copies:
        copy.wait()


def final_kernel(k_ref, v_ref, kp_ref, vp_ref, kept_ref, got_ref, tail_ref, *rest, group):
    kg_hbm, vg_hbm, kg_ref, vg_ref, sems = rest[-5:]
    width = k_ref.shape[1]
    pairs = width // PAIR
    tail = tail_ref[...]
    copies = []
    for pair in range(pairs):
        for h, later in zip((2 * pair, 2 * pair + 1), get_states(pair, pairs, kept_ref, got_ref)):
            c = head(h)
            kg_ref[:, c] = (kp_ref[:, c] + dot(v_ref[:, c] * tail, later, 1, 1)).astype(BF16)
            vg_ref[:, c] = (vp_ref[:, c] + dot(k_ref[:, c] * tail, later, 1, 0)).astype(BF16)
        for i, (source, target) in enumerate(((kg_ref, kg_hbm), (vg_ref, vg_hbm))):
            copy = pltpu.make_async_copy(
                source.at[:, both(pair)],
                target.at[:, pl.ds(group * width + pair * PAIR, PAIR)],
                sems.at[pair, i],
            )
            copy.start()
            copies.append(copy)
    for copy in copies:
        copy.wait()


def swap(block, distance):
    count = lax.axis_size("ctx")
    return lax.ppermute(block, "ctx", [(i, i ^ distance) for i in range(count)])


def scan(keep, send, bits, backward):
    count = lax.axis_size("ctx")
    rows = keep.shape[0]
    half = rows // 2

    def last(distance):
        row = FLAG * (distance.bit_length() - 1)
        bit = bits[row : row + 1]
        return bit < 0.5 if backward else bit > 0.5

    def packed(block, flag, extra):
        return jnp.concatenate([block, jnp.broadcast_to(flag, (FLAG, E)), extra])

    got = yield send, 1
    flag, got_flag = send[rows : rows + 1], got[rows : rows + 1]
    extra = send[rows + FLAG :] + got[rows + FLAG :]
    second = last(1)
    first_core = jnp.where(second, got[:rows], keep)
    core_flag = jnp.where(second, got_flag, flag)
    late_flag = jnp.where(second, flag, got_flag)

    def both_cores(part):
        mine, other = keep[part], got[part]
        return jnp.where(second, mine, other) + (1.0 - late_flag) * jnp.where(second, other, mine)

    flag = jnp.maximum(flag, got_flag)

    block = packed(both_cores(slice(half, rows)), flag, extra)
    keep = both_cores(slice(0, half))
    got = yield block, 2
    got_flag = got[half : half + 1]
    extra = extra + got[half + FLAG :]
    second = last(2)
    first_chip = jnp.where(second, got[:half], keep)
    chip_flag = jnp.where(second, got_flag, flag)
    late, late_flag = jnp.where(second, keep, got[:half]), jnp.where(second, flag, got_flag)
    total = late + (1.0 - late_flag) * first_chip
    flag = jnp.maximum(flag, got_flag)

    before, before_flag = jnp.zeros_like(total), jnp.zeros_like(flag)
    distance = 4
    while distance < count:
        got = yield packed(total, flag, extra), distance
        got_total, got_flag = got[:half], got[half : half + 1]
        extra = extra + got[half + FLAG :]
        second = last(distance)
        before = jnp.where(second, before + (1.0 - before_flag) * got_total, before)
        before_flag = jnp.where(second, jnp.maximum(before_flag, got_flag), before_flag)
        total = jnp.where(
            second, total + (1.0 - flag) * got_total, got_total + (1.0 - got_flag) * total
        )
        flag = jnp.maximum(flag, got_flag)
        distance *= 2

    after = first_chip + (1.0 - chip_flag) * before
    second = last(2)
    mine, theirs = jnp.where(second, after, before), jnp.where(second, before, after)
    got = yield theirs, 2
    before = jnp.concatenate([mine, got])
    after = first_core + (1.0 - core_flag) * before
    second = last(1)
    mine, theirs = jnp.where(second, after, before), jnp.where(second, before, after)
    got = yield theirs, 1
    return mine, got, extra


def rounds(one, two, work):
    chains, waiting, results, pending = [one], {}, {}, ()
    number = 0
    while chains:
        if number == 1:
            chains.append(two)
        for chain in chains:
            if chain not in waiting:
                waiting[chain] = next(chain)
        blocks, _ = lax.optimization_barrier(([waiting[c][0] for c in chains], pending))
        pending = work[number](blocks[0]) if number in work else ()
        for chain, block in zip(list(chains), blocks):
            try:
                waiting[chain] = chain.send(swap(block, waiting[chain][1]))
            except StopIteration as end:
                results[chain] = end.value
                chains.remove(chain)
        number += 1
    return results[one], results[two]


def shards(queries, key_vectors, value_vectors, out_grad, norm_gain, doc_bounds):
    tokens, width = queries.shape
    groups = range(2)
    half = width // 2
    pairs = half // PAIR
    rows = pairs * E
    extra = rows + FLAG + 2 * pairs
    queries, key_vectors, value_vectors, out_grad, gains, doc_bounds = (
        pltpu.with_memory_space_constraint(x, pltpu.HBM)
        for x in (
            queries, key_vectors, value_vectors, out_grad, norm_gain.reshape(1, width), doc_bounds
        )
    )

    def shape(count, columns, dtype=F32):
        return jax.ShapeDtypeStruct((count, columns), dtype)

    def call(kernel, inputs, outputs, scratch=(), aliases={}, **sizes):
        return pl.pallas_call(
            functools.partial(kernel, **sizes),
            in_specs=inputs,
            out_specs=[spec for spec, _ in outputs],
            out_shape=[out for _, out in outputs],
            scratch_shapes=scratch,
            input_output_aliases=aliases,
            compiler_params=pltpu.CompilerParams(vmem_limit_bytes=VMEM_LIMIT),
        )

    def copies(*counts):
        return pltpu.SemaphoreType.DMA(counts)

    levels = lax.axis_size("ctx").bit_length() - 1
    narrow, single = (VMEM, shape(tokens, half, BF16)), (VMEM, shape(tokens, half))
    staging = pltpu.VMEM((tokens, half), BF16)
    states = [(VMEM, shape(rows, E)), (VMEM, shape(rows + FLAG, E))]
    local, carried, middle, spread = {}, {}, {}, {}
    *first, key, value, start, end, use, tail, flag, bits = call(
        first_state_kernel,
        [ANY] * 3,
        states + [narrow] * 2 + [(VMEM, shape(tokens, E, jnp.int32))] * 2
        + [(VMEM, shape(tokens, E, BF16))] * 2
        + [(VMEM, shape(FLAG, E)), (VMEM, shape(FLAG * levels, E))],
        [pltpu.SMEM(doc_bounds.shape, jnp.int32), copies(pairs, 2), copies()],
        group=0,
    )(doc_bounds, key_vectors, value_vectors)
    *second, other_key, other_value = call(
        state_kernel, [ANY] * 2 + [VMEM] * 2, states + [narrow] * 2, [copies(pairs, 2)], group=1
    )(key_vectors, value_vectors, tail, flag)
    keys, values = (key, other_key), (value, other_value)

    def local_of(g, token):
        local[g] = call(
            local_kernel,
            [ANY] * 3 + [VMEM] * 3 + [ANY],
            [single, narrow, narrow, (VMEM, shape(1, half))],
            [copies(pairs, 2), copies()],
            group=g,
        )(queries, out_grad, gains, keys[g], values[g], start, token)
        return local[g][0]

    def spread_of(g, token):
        done = spread[0][:1] if g else []
        spread[g] = call(
            spread_kernel,
            [VMEM] * 9 + [ANY] * (1 + len(done)),
            [(ANY, shape(tokens, width, BF16)), single, single],
            [staging, copies(pairs)],
            {10: 0} if done else {},
            group=g,
        )(
            local[g][1], keys[g], values[g], middle[g], *carried[g],
            use, start, end, token, *done,
        )
        return spread[g][1]

    def chain(g, state):
        *carried[g], _ = yield from scan(*state, bits, False)
        middle[g], *state = call(
            middle_kernel,
            [VMEM] * 8,
            [narrow, (VMEM, shape(rows, E)), (VMEM, shape(extra, E))],
        )(*local[g][1:], local[g][0], *carried[g], use, flag)
        return (yield from scan(*state, bits, True))

    count = levels + 2
    later = rounds(
        chain(0, first),
        chain(1, second),
        {
            1: functools.partial(local_of, 0),
            3: functools.partial(local_of, 1),
            count + 1: functools.partial(spread_of, 0),
            count + 3: functools.partial(spread_of, 1),
        },
    )
    grads = ()
    for g in groups:
        grads = call(
            final_kernel,
            [VMEM] * 7 + [ANY] * len(grads),
            [(ANY, shape(tokens, width, BF16))] * 2,
            [staging, staging, copies(pairs, 2)],
            {7: 0, 8: 1} if grads else {},
            group=g,
        )(keys[g], values[g], *spread[g][1:], *later[g][:2], tail, *grads)
    total = jnp.concatenate([later[g][2] for g in groups])
    gain_grad = total.reshape(width) / math.sqrt(tokens * lax.axis_size("ctx"))
    return spread[1][0], *grads, gain_grad


def solution(mesh):
    tokens = P(("parts", "ctx"), None)
    return jax.shard_map(
        shards,
        mesh=mesh,
        in_specs=(tokens, tokens, tokens, tokens, P(), P(None, ("parts", "ctx"))),
        out_specs=(tokens, tokens, tokens, P("parts")),
        check_vma=False,
    )
```

```python
import functools
import math

import jax
import jax.numpy as jnp
from jax import lax
from jax.experimental import pallas as pl
from jax.experimental.pallas import tpu as pltpu
from jax.sharding import PartitionSpec as P

E = 128
PAIR = 2 * E
FLAG = 8
SQUARE = 4
EPS = 1e-06
VMEM_LIMIT = 8 * 1024 * 1024
F32 = jnp.float32
BF16 = jnp.bfloat16
VMEM = pl.BlockSpec(memory_space=pltpu.VMEM)
ANY = pl.BlockSpec(memory_space=pl.ANY)


def dot(a, b, a_dim, b_dim):
    return lax.dot_general(a, b, (((a_dim,), (b_dim,)), ((), ())), preferred_element_type=F32)


def head(h):
    return slice(h * E, (h + 1) * E)


def both(pair):
    return slice(pair * PAIR, (pair + 1) * PAIR)


def place(pair, pairs):
    chip = (lax.axis_index("ctx") // 2) % SQUARE
    slot = ((pair % SQUARE) ^ chip) * (pairs // SQUARE) + pair // SQUARE
    return pl.ds(pl.multiple_of(slot * E, E), E)


def put_states(states, pair, pairs, keep_ref, send_ref):
    where = place(pair, pairs)
    core = lax.axis_index("ctx") % 2
    keep_ref[where, :] = jnp.where(core == 0, states[0], states[1])
    send_ref[where, :] = jnp.where(core == 0, states[1], states[0])


def get_states(pair, pairs, kept_ref, got_ref):
    where = place(pair, pairs)
    core = lax.axis_index("ctx") % 2
    kept, got = kept_ref[where, :], got_ref[where, :]
    return (
        jnp.where(core == 0, kept, got).astype(BF16),
        jnp.where(core == 0, got, kept).astype(BF16),
    )


def fetch(group, sources, targets, sems):
    width = targets[0].shape[1]
    copies = []
    for pair in range(width // PAIR):
        copies.append([])
        for i, (source, target) in enumerate(zip(sources, targets)):
            copy = pltpu.make_async_copy(
                source.at[:, pl.ds(group * width + pair * PAIR, PAIR)],
                target.at[:, both(pair)],
                sems.at[pair, i],
            )
            copy.start()
            copies[-1].append(copy)
    return copies


def row_values(values, rows, dtype):
    position = lax.broadcasted_iota(jnp.int32, (rows, E), 0)
    result = jnp.full((rows, E), values[0])
    for block in range(1, len(values)):
        result = jnp.where(position >= block * (rows // len(values)), values[block], result)
    return result.astype(dtype)


def states_of(k_ref, v_ref, tail_ref, copies, keep_ref, send_ref):
    pairs = len(copies)
    tail = tail_ref[...]
    for pair in range(pairs):
        for copy in copies[pair]:
            copy.wait()
        states = [
            dot(k_ref[:, head(h)] * tail, v_ref[:, head(h)], 0, 0) for h in (2 * pair, 2 * pair + 1)
        ]
        put_states(states, pair, pairs, keep_ref, send_ref)


def first_state_kernel(
    bounds_hbm, k_hbm, v_hbm,
    keep_ref, send_ref, k_ref, v_ref, start_ref, end_ref, use_ref, tail_ref, flag_ref, bits_ref,
    bounds, sems, bounds_sem, *, group,
):
    bounds_copy = pltpu.make_async_copy(bounds_hbm, bounds, bounds_sem)
    bounds_copy.start()
    copies = fetch(group, (k_hbm, v_hbm), (k_ref, v_ref), sems)
    rows, width = k_ref.shape
    count = bounds.shape[1]
    block_len = rows // count
    me = lax.axis_index("ctx")
    first = me * count
    for bit in range(bits_ref.shape[0] // FLAG):
        value = jnp.full((FLAG, E), (me // 2**bit) % 2)
        bits_ref[bit * FLAG : (bit + 1) * FLAG, :] = value.astype(F32)
    bounds_copy.wait()
    opens = [bounds[0, b] for b in range(count)]
    closes = [bounds[1, b] for b in range(count)]
    flag = jnp.full((FLAG, E), (opens[-1] >= first).astype(F32))
    flag_ref[...] = flag
    send_ref[width // 2 :, :] = flag
    use_ref[...] = row_values([(x < first).astype(F32) for x in opens], rows, BF16)
    tail_ref[...] = row_values([(x >= first + count - 1).astype(F32) for x in closes], rows, BF16)
    start_ref[...] = row_values([(x - first) * block_len for x in opens], rows, jnp.int32)
    end_ref[...] = row_values([(x - first + 1) * block_len for x in closes], rows, jnp.int32)
    states_of(k_ref, v_ref, tail_ref, copies, keep_ref, send_ref)


def state_kernel(
    k_hbm, v_hbm, tail_ref, flag_ref, keep_ref, send_ref, k_ref, v_ref, sems, *, group
):
    copies = fetch(group, (k_hbm, v_hbm), (k_ref, v_ref), sems)
    send_ref[k_ref.shape[1] // 2 :, :] = flag_ref[...]
    states_of(k_ref, v_ref, tail_ref, copies, keep_ref, send_ref)


def sight(bound_ref, turned):
    rows = bound_ref.shape[0]
    row = lax.broadcasted_iota(jnp.int32, (rows, E), 0)
    parts = []
    for c in range(rows // E):
        column = lax.broadcasted_iota(jnp.int32, (rows, E), 1) + c * E
        if turned:
            seen = (column >= row) & (column < bound_ref[...])
        else:
            seen = (column <= row) & (column >= bound_ref[...])
        parts.append(jnp.where(seen, 1.0, 0.0).astype(BF16))
    return jnp.concatenate(parts, axis=1)


def local_kernel(
    q_hbm, g_hbm, gain_hbm, k_ref, v_ref, start_ref, _,
    out_ref, q_ref, g_ref, gain_ref, sems, gain_sem, *, group,
):
    width = k_ref.shape[1]
    copies = fetch(group, (q_hbm, g_hbm), (q_ref, g_ref), sems)
    gain_copy = pltpu.make_async_copy(
        gain_hbm.at[:, pl.ds(group * width, width)], gain_ref, gain_sem
    )
    gain_copy.start()
    mask = sight(start_ref, False)
    for pair in range(width // PAIR):
        copies[pair][0].wait()
        for h in (2 * pair, 2 * pair + 1):
            scores = dot(q_ref[:, head(h)], k_ref[:, head(h)], 1, 1).astype(BF16) * mask
            out_ref[:, head(h)] = dot(scores, v_ref[:, head(h)], 1, 0)
    for pair in range(width // PAIR):
        copies[pair][1].wait()
    gain_copy.wait()


def middle_kernel(
    q_ref, g_ref, gain_ref, local_ref, kept_ref, got_ref, use_ref, flag_ref,
    d_ref, keep_ref, send_ref,
):
    pairs = q_ref.shape[1] // PAIR
    use = use_ref[...]
    send_ref[pairs * E : pairs * E + FLAG, :] = flag_ref[...]
    for pair in range(pairs):
        states = []
        for h, carry in zip((2 * pair, 2 * pair + 1), get_states(pair, pairs, kept_ref, got_ref)):
            used = q_ref[:, head(h)] * use
            attended = local_ref[:, head(h)] + dot(used, carry, 1, 0)
            inverse = lax.rsqrt(jnp.mean(attended * attended, axis=1, keepdims=True) + EPS)
            normed = attended * inverse
            grad = g_ref[:, head(h)].astype(F32)
            gained = grad * normed
            row = pairs * E + FLAG + h
            send_ref[row : row + 1, :] = jnp.sum(gained, axis=0, keepdims=True)
            gain = gain_ref[:, head(h)]
            centre = jnp.mean(gained * gain, axis=1, keepdims=True)
            d_att = ((grad * gain - normed * centre) * inverse).astype(BF16)
            d_ref[:, head(h)] = d_att
            states.append(dot(used, d_att, 0, 0))
        put_states(states, pair, pairs, keep_ref, send_ref)


def spread_kernel(
    q_ref, k_ref, v_ref, d_ref, kept_ref, got_ref, use_ref, start_ref, end_ref, *rest, group
):
    qg_hbm, kp_ref, vp_ref, qg_ref, sems = rest[-5:]
    width = q_ref.shape[1]
    pairs = width // PAIR
    use = use_ref[...]
    mask = sight(start_ref, False)
    turned_mask = sight(end_ref, True)
    copies = []
    for pair in range(pairs):
        for h, carry in zip((2 * pair, 2 * pair + 1), get_states(pair, pairs, kept_ref, got_ref)):
            c = head(h)
            query, key, value, d_att = q_ref[:, c], k_ref[:, c], v_ref[:, c], d_ref[:, c]
            dscores = dot(d_att, value, 1, 1).astype(BF16) * mask
            from_carry = dot(d_att * use, carry, 1, 1)
            qg_ref[:, c] = (dot(dscores, key, 1, 0) + from_carry).astype(BF16)
            turned = dot(value, d_att, 1, 1).astype(BF16) * turned_mask
            kp_ref[:, c] = dot(turned, query, 1, 0)
            turned = dot(key, query, 1, 1).astype(BF16) * turned_mask
            vp_ref[:, c] = dot(turned, d_att, 1, 0)
        copy = pltpu.make_async_copy(
            qg_ref.at[:, both(pair)],
            qg_hbm.at[:, pl.ds(group * width + pair * PAIR, PAIR)],
            sems.at[pair],
        )
        copy.start()
        copies.append(copy)
    for copy in copies:
        copy.wait()


def final_kernel(k_ref, v_ref, kp_ref, vp_ref, kept_ref, got_ref, tail_ref, *rest, group):
    kg_hbm, vg_hbm, kg_ref, vg_ref, sems = rest[-5:]
    width = k_ref.shape[1]
    pairs = width // PAIR
    tail = tail_ref[...]
    copies = []
    for pair in range(pairs):
        for h, later in zip((2 * pair, 2 * pair + 1), get_states(pair, pairs, kept_ref, got_ref)):
            c = head(h)
            kg_ref[:, c] = (kp_ref[:, c] + dot(v_ref[:, c] * tail, later, 1, 1)).astype(BF16)
            vg_ref[:, c] = (vp_ref[:, c] + dot(k_ref[:, c] * tail, later, 1, 0)).astype(BF16)
        for i, (source, target) in enumerate(((kg_ref, kg_hbm), (vg_ref, vg_hbm))):
            copy = pltpu.make_async_copy(
                source.at[:, both(pair)],
                target.at[:, pl.ds(group * width + pair * PAIR, PAIR)],
                sems.at[pair, i],
            )
            copy.start()
            copies.append(copy)
    for copy in copies:
        copy.wait()


def swap(block, distance):
    count = lax.axis_size("ctx")
    return lax.ppermute(block, "ctx", [(i, i ^ distance) for i in range(count)])


def combine(early, late):
    return jnp.maximum(early[0], late[0]), late[1] + (1.0 - late[0]) * early[1]


def crossed(bit, zero, one):
    return jnp.where(bit, one, zero), jnp.where(bit, zero, one)


def permuted(parts, low, high):
    a, b = crossed(low, parts[0], parts[1])
    c, d = crossed(low, parts[2], parts[3])
    a, c = crossed(high, a, c)
    b, d = crossed(high, b, d)
    return [a, b, c, d]


def scan(keep, send, bits, backward):
    count = lax.axis_size("ctx")
    rows = keep.shape[0]
    part = rows // SQUARE

    def last(distance):
        row = FLAG * (distance.bit_length() - 1)
        bit = bits[row : row + 1]
        return bit < 0.5 if backward else bit > 0.5

    def packed(block, flag, extra):
        return jnp.concatenate([block, jnp.broadcast_to(flag, (FLAG, E)), extra])

    (got,) = yield [(send, 1)]
    core_flag, late_flag = crossed(last(1), send[rows : rows + 1], got[rows : rows + 1])
    extra = send[rows + FLAG :] + got[rows + FLAG :]
    first_core = jnp.where(last(1), got[:rows], keep)
    flag = jnp.maximum(core_flag, late_flag)

    def both_cores(number):
        where = slice(number * part, (number + 1) * part)
        early, late = crossed(last(1), keep[where], got[where])
        return late + (1.0 - late_flag) * early

    gots = yield [
        (packed(both_cores(number), flag, extra), 2 * number) for number in range(1, SQUARE)
    ]
    extra = sum((got[part + FLAG :] for got in gots), extra)
    flags = permuted([flag] + [got[part : part + 1] for got in gots], last(2), last(4))
    sums = permuted([both_cores(0)] + [got[:part] for got in gots], last(2), last(4))
    runs = [(flags[0], sums[0])]
    for following in list(zip(flags, sums))[1:]:
        runs.append(combine(runs[-1], following))
    flag, total = runs.pop()

    before = jnp.zeros_like(flag), jnp.zeros_like(total)
    distance = 2 * SQUARE
    while distance < count:
        (got,) = yield [(packed(total, flag, extra), distance)]
        extra = extra + got[part + FLAG :]
        got = got[part : part + 1], got[:part]
        longer = combine(got, before)
        before = [jnp.where(last(distance), new, old) for new, old in zip(longer, before)]
        after, ahead = combine((flag, total), got), combine(got, (flag, total))
        flag, total = (jnp.where(last(distance), b, a) for a, b in zip(after, ahead))
        distance *= 2

    results = [before[1]] + [combine(before, run)[1] for run in runs]
    results = permuted(results, last(2), last(4))
    gots = yield [(results[number], 2 * number) for number in range(1, SQUARE)]
    before = jnp.concatenate([results[0], *gots])
    after = first_core + (1.0 - core_flag) * before
    mine, theirs = crossed(last(1), before, after)
    (got,) = yield [(theirs, 1)]
    return mine, got, extra


def run(chain, work):
    swaps = next(chain)
    number, done = 0, ()
    while True:
        blocks, _ = lax.optimization_barrier(([block for block, _ in swaps], done))
        done = work[number](blocks[0]) if number in work else ()
        try:
            swaps = chain.send([swap(b, distance) for b, (_, distance) in zip(blocks, swaps)])
        except StopIteration as end:
            return end.value
        number += 1


def shards(queries, key_vectors, value_vectors, out_grad, norm_gain, doc_bounds):
    tokens, width = queries.shape
    groups = range(1)
    half = width
    pairs = half // PAIR
    rows = pairs * E
    extra = rows + FLAG + 2 * pairs
    queries, key_vectors, value_vectors, out_grad, gains, doc_bounds = (
        pltpu.with_memory_space_constraint(x, pltpu.HBM)
        for x in (
            queries, key_vectors, value_vectors, out_grad, norm_gain.reshape(1, width), doc_bounds
        )
    )

    def shape(count, columns, dtype=F32):
        return jax.ShapeDtypeStruct((count, columns), dtype)

    def call(kernel, inputs, outputs, scratch=(), aliases={}, **sizes):
        return pl.pallas_call(
            functools.partial(kernel, **sizes),
            in_specs=inputs,
            out_specs=[spec for spec, _ in outputs],
            out_shape=[out for _, out in outputs],
            scratch_shapes=scratch,
            input_output_aliases=aliases,
            compiler_params=pltpu.CompilerParams(vmem_limit_bytes=VMEM_LIMIT),
        )

    def copies(*counts):
        return pltpu.SemaphoreType.DMA(counts)

    levels = lax.axis_size("ctx").bit_length() - 1
    narrow, single = (VMEM, shape(tokens, half, BF16)), (VMEM, shape(tokens, half))
    staging = pltpu.VMEM((tokens, half), BF16)
    states = [(VMEM, shape(rows, E)), (VMEM, shape(rows + FLAG, E))]
    local, carried, middle, spread = {}, {}, {}, {}
    *first, key, value, start, end, use, tail, flag, bits = call(
        first_state_kernel,
        [ANY] * 3,
        states + [narrow] * 2 + [(VMEM, shape(tokens, E, jnp.int32))] * 2
        + [(VMEM, shape(tokens, E, BF16))] * 2
        + [(VMEM, shape(FLAG, E)), (VMEM, shape(FLAG * levels, E))],
        [pltpu.SMEM(doc_bounds.shape, jnp.int32), copies(pairs, 2), copies()],
        group=0,
    )(doc_bounds, key_vectors, value_vectors)
    keys, values = (key,), (value,)

    def local_of(g, token):
        local[g] = call(
            local_kernel,
            [ANY] * 3 + [VMEM] * 3 + [ANY],
            [single, narrow, narrow, (VMEM, shape(1, half))],
            [copies(pairs, 2), copies()],
            group=g,
        )(queries, out_grad, gains, keys[g], values[g], start, token)
        return local[g][0]

    def spread_of(g, token):
        done = spread[0][:1] if g else []
        spread[g] = call(
            spread_kernel,
            [VMEM] * 9 + [ANY] * (1 + len(done)),
            [(ANY, shape(tokens, width, BF16)), single, single],
            [staging, copies(pairs)],
            {10: 0} if done else {},
            group=g,
        )(
            local[g][1], keys[g], values[g], middle[g], *carried[g],
            use, start, end, token, *done,
        )
        return spread[g][1]

    def chain(g, state):
        *carried[g], _ = yield from scan(*state, bits, False)
        middle[g], *state = call(
            middle_kernel,
            [VMEM] * 8,
            [narrow, (VMEM, shape(rows, E)), (VMEM, shape(extra, E))],
        )(*local[g][1:], local[g][0], *carried[g], use, flag)
        return (yield from scan(*state, bits, True))

    steps = levels + 1
    longest = steps - 3
    later = [
        run(
            chain(g, first),
            {
                longest: functools.partial(local_of, g),
                steps + longest: functools.partial(spread_of, g),
            },
        )
        for g in groups
    ]
    grads = ()
    for g in groups:
        grads = call(
            final_kernel,
            [VMEM] * 7 + [ANY] * len(grads),
            [(ANY, shape(tokens, width, BF16))] * 2,
            [staging, staging, copies(pairs, 2)],
            {7: 0, 8: 1} if grads else {},
            group=g,
        )(keys[g], values[g], *spread[g][1:], *later[g][:2], tail, *grads)
    total = jnp.concatenate([later[g][2] for g in groups])
    gain_grad = total.reshape(width) / math.sqrt(tokens * lax.axis_size("ctx"))
    return spread[0][0], *grads, gain_grad


def solution(mesh):
    tokens = P(("parts", "ctx"), None)
    return jax.shard_map(
        shards,
        mesh=mesh,
        in_specs=(tokens, tokens, tokens, tokens, P(), P(None, ("parts", "ctx"))),
        out_specs=(tokens, tokens, tokens, P("parts")),
        check_vma=False,
    )
```

```python
import functools
import math

import jax
import jax.numpy as jnp
from jax import lax
from jax.experimental import pallas as pl
from jax.experimental.pallas import tpu as pltpu
from jax.sharding import PartitionSpec as P

E = 128
PAIR = 2 * E
FLAG = 8
SQUARE = 4
TOGETHER = 4
EPS = 1e-06
VMEM_LIMIT = 8 * 1024 * 1024
F32 = jnp.float32
BF16 = jnp.bfloat16
VMEM = pl.BlockSpec(memory_space=pltpu.VMEM)
ANY = pl.BlockSpec(memory_space=pl.ANY)


def dot(a, b, a_dim, b_dim):
    return lax.dot_general(a, b, (((a_dim,), (b_dim,)), ((), ())), preferred_element_type=F32)


def head(h):
    return slice(h * E, (h + 1) * E)


def place(pair, pairs):
    chip = (lax.axis_index("ctx") // 2) % SQUARE
    slot = ((pair % SQUARE) ^ chip) * (pairs // SQUARE) + pair // SQUARE
    return pl.ds(pl.multiple_of(slot * E, E), E)


def owner_column(pair, other):
    core = lax.axis_index("ctx") % 2
    return pl.ds(pl.multiple_of((2 * pair + (core + other) % 2) * E, E), E)


def fetch(other, sources, targets, sems):
    copies = []
    for pair in range(targets[0].shape[1] // E):
        copies.append([])
        for i, (source, target) in enumerate(zip(sources, targets)):
            copy = pltpu.make_async_copy(
                source.at[:, owner_column(pair, other)], target.at[:, head(pair)], sems.at[pair, i]
            )
            copy.start()
            copies[-1].append(copy)
    return copies


def put(source, target, pair, other, sem):
    copy = pltpu.make_async_copy(
        source.at[:, head(pair)], target.at[:, owner_column(pair, other)], sem
    )
    copy.start()
    return copy


def row_values(values, rows, dtype):
    position = lax.broadcasted_iota(jnp.int32, (rows, E), 0)
    result = jnp.full((rows, E), values[0])
    for block in range(1, len(values)):
        result = jnp.where(position >= block * (rows // len(values)), values[block], result)
    return result.astype(dtype)


def states_of(k_ref, v_ref, tail_ref, copies, out_ref):
    pairs = len(copies)
    for begin in range(0, pairs, TOGETHER):
        together = range(begin, min(begin + TOGETHER, pairs))
        for pair in together:
            for copy in copies[pair]:
                copy.wait()
        for pair in together:
            state = dot(k_ref[:, head(pair)] * tail_ref[...], v_ref[:, head(pair)], 0, 0)
            out_ref[place(pair, pairs), :] = state


def send_state_kernel(
    bounds_hbm, k_hbm, v_hbm,
    send_ref, k_ref, v_ref, start_ref, end_ref, use_ref, tail_ref, flag_ref, bits_ref,
    bounds, sems, bounds_sem,
):
    bounds_copy = pltpu.make_async_copy(bounds_hbm, bounds, bounds_sem)
    bounds_copy.start()
    copies = fetch(1, (k_hbm, v_hbm), (k_ref, v_ref), sems)
    rows, width = k_ref.shape
    count = bounds.shape[1]
    block_len = rows // count
    me = lax.axis_index("ctx")
    first = me * count
    for bit in range(bits_ref.shape[0] // FLAG):
        value = jnp.full((FLAG, E), (me // 2**bit) % 2)
        bits_ref[bit * FLAG : (bit + 1) * FLAG, :] = value.astype(F32)
    bounds_copy.wait()
    opens = [bounds[0, b] for b in range(count)]
    closes = [bounds[1, b] for b in range(count)]
    flag = jnp.full((FLAG, E), (opens[-1] >= first).astype(F32))
    flag_ref[...] = flag
    send_ref[width:, :] = flag
    use_ref[...] = row_values([(x < first).astype(F32) for x in opens], rows, BF16)
    tail_ref[...] = row_values([(x >= first + count - 1).astype(F32) for x in closes], rows, BF16)
    start_ref[...] = row_values([(x - first) * block_len for x in opens], rows, jnp.int32)
    end_ref[...] = row_values([(x - first + 1) * block_len for x in closes], rows, jnp.int32)
    states_of(k_ref, v_ref, tail_ref, copies, send_ref)


def keep_state_kernel(k_hbm, v_hbm, tail_ref, keep_ref, k_ref, v_ref, sems):
    copies = fetch(0, (k_hbm, v_hbm), (k_ref, v_ref), sems)
    states_of(k_ref, v_ref, tail_ref, copies, keep_ref)


def sight(bound_ref, turned):
    rows = bound_ref.shape[0]
    row = lax.broadcasted_iota(jnp.int32, (rows, E), 0)
    parts = []
    for c in range(rows // E):
        column = lax.broadcasted_iota(jnp.int32, (rows, E), 1) + c * E
        if turned:
            seen = (column >= row) & (column < bound_ref[...])
        else:
            seen = (column <= row) & (column >= bound_ref[...])
        parts.append(jnp.where(seen, 1.0, 0.0).astype(BF16))
    return jnp.concatenate(parts, axis=1)


def local_kernel(
    q_hbm, g_hbm, gain_hbm, k_ref, v_ref, start_ref, _,
    out_ref, q_ref, g_ref, gain_ref, q_sems, g_sems, gain_sem, *, other,
):
    copies = fetch(other, [q_hbm], [q_ref], q_sems)
    grad_copies = fetch(other, [g_hbm], [g_ref], g_sems)
    gain_copy = pltpu.make_async_copy(gain_hbm, gain_ref, gain_sem)
    gain_copy.start()
    mask = sight(start_ref, False)
    pairs = len(copies)
    for begin in range(0, pairs, TOGETHER):
        together = range(begin, min(begin + TOGETHER, pairs))
        for pair in together:
            copies[pair][0].wait()
        for pair in together:
            c = head(pair)
            scores = dot(q_ref[:, c], k_ref[:, c], 1, 1).astype(BF16) * mask
            out_ref[:, c] = dot(scores, v_ref[:, c], 1, 0)
    for (copy,) in grad_copies:
        copy.wait()
    gain_copy.wait()


def middle_kernel(q_ref, g_ref, gain_ref, local_ref, carry_ref, use_ref, *rest, other):
    if other:
        flag_ref, sums_ref, d_ref, state_ref = rest
    else:
        d_ref, state_ref, sums_ref = rest
    pairs = q_ref.shape[1] // E
    use = use_ref[...]
    core = lax.axis_index("ctx") % 2
    for pair in range(pairs):
        c = head(pair)
        used = q_ref[:, c] * use
        carry = carry_ref[place(pair, pairs), :].astype(BF16)
        attended = local_ref[:, c] + dot(used, carry, 1, 0)
        inverse = lax.rsqrt(jnp.mean(attended * attended, axis=1, keepdims=True) + EPS)
        normed = attended * inverse
        grad = g_ref[:, c].astype(F32)
        gained = grad * normed
        gain = gain_ref[:, owner_column(pair, other)]
        centre = jnp.mean(gained * gain, axis=1, keepdims=True)
        d_att = ((grad * gain - normed * centre) * inverse).astype(BF16)
        d_ref[:, c] = d_att
        state_ref[place(pair, pairs), :] = dot(used, d_att, 0, 0)
        total = jnp.sum(gained, axis=0, keepdims=True)
        if other:
            both = jnp.concatenate(
                crossed(core == 0, total, sums_ref[pair : pair + 1, :])
            )
            begin = pairs * E + FLAG + 2 * pair
            state_ref[begin : begin + 2, :] = both
        else:
            sums_ref[pair : pair + 1, :] = total
    if other:
        state_ref[pairs * E : pairs * E + FLAG, :] = flag_ref[...]


def spread_kernel(
    q_ref, k_ref, v_ref, d_ref, carry_ref, use_ref, start_ref, end_ref, *rest, other
):
    qg_hbm, kp_ref, vp_ref, qg_ref, sems = rest[-5:]
    pairs = q_ref.shape[1] // E
    use = use_ref[...]
    mask = sight(start_ref, False)
    turned_mask = sight(end_ref, True)
    copies = []
    for pair in range(pairs):
        c = head(pair)
        carry = carry_ref[place(pair, pairs), :].astype(BF16)
        query, key, value, d_att = q_ref[:, c], k_ref[:, c], v_ref[:, c], d_ref[:, c]
        dscores = dot(d_att, value, 1, 1).astype(BF16) * mask
        from_carry = dot(d_att * use, carry, 1, 1)
        qg_ref[:, c] = (dot(dscores, key, 1, 0) + from_carry).astype(BF16)
        turned = dot(value, d_att, 1, 1).astype(BF16) * turned_mask
        kp_ref[:, c] = dot(turned, query, 1, 0)
        turned = dot(key, query, 1, 1).astype(BF16) * turned_mask
        vp_ref[:, c] = dot(turned, d_att, 1, 0)
        copies.append(put(qg_ref, qg_hbm, pair, other, sems.at[pair]))
    for copy in copies:
        copy.wait()


def final_kernel(k_ref, v_ref, kp_ref, vp_ref, later_ref, tail_ref, *rest, other):
    kg_hbm, vg_hbm, kg_ref, vg_ref, sems = rest[-5:]
    pairs = k_ref.shape[1] // E
    tail = tail_ref[...]
    copies = []
    for pair in range(pairs):
        c = head(pair)
        later = later_ref[place(pair, pairs), :].astype(BF16)
        kg_ref[:, c] = (kp_ref[:, c] + dot(v_ref[:, c] * tail, later, 1, 1)).astype(BF16)
        vg_ref[:, c] = (vp_ref[:, c] + dot(k_ref[:, c] * tail, later, 1, 0)).astype(BF16)
        copies.append(put(kg_ref, kg_hbm, pair, other, sems.at[pair, 0]))
        copies.append(put(vg_ref, vg_hbm, pair, other, sems.at[pair, 1]))
    for copy in copies:
        copy.wait()


def swap(block, distance):
    count = lax.axis_size("ctx")
    return lax.ppermute(block, "ctx", [(i, i ^ distance) for i in range(count)])


def combine(early, late):
    return jnp.maximum(early[0], late[0]), late[1] + (1.0 - late[0]) * early[1]


def crossed(bit, zero, one):
    return jnp.where(bit, one, zero), jnp.where(bit, zero, one)


def permuted(parts, low, high):
    a, b = crossed(low, parts[0], parts[1])
    c, d = crossed(low, parts[2], parts[3])
    a, c = crossed(high, a, c)
    b, d = crossed(high, b, d)
    return [a, b, c, d]


def scan(keep, send, bits, backward, early):
    count = lax.axis_size("ctx")
    rows = keep.shape[0]
    part = rows // SQUARE

    def last(distance):
        row = FLAG * (distance.bit_length() - 1)
        bit = bits[row : row + 1]
        return bit < 0.5 if backward else bit > 0.5

    def packed(block, flag, extra):
        return jnp.concatenate([block, jnp.broadcast_to(flag, (FLAG, E)), extra])

    (got,) = yield [(send, 1)]
    core_flag, late_flag = crossed(last(1), send[rows : rows + 1], got[rows : rows + 1])
    extra = send[rows + FLAG :] + got[rows + FLAG :]
    first_core = jnp.where(last(1), got[:rows], keep)
    flag = jnp.maximum(core_flag, late_flag)

    def both_cores(number):
        where = slice(number * part, (number + 1) * part)
        early, late = crossed(last(1), keep[where], got[where])
        return late + (1.0 - late_flag) * early

    gots = yield [
        (packed(both_cores(number), flag, extra), 2 * number) for number in range(1, SQUARE)
    ]
    extra = sum((got[part + FLAG :] for got in gots), extra)
    flags = permuted([flag] + [got[part : part + 1] for got in gots], last(2), last(4))
    sums = permuted([both_cores(0)] + [got[:part] for got in gots], last(2), last(4))
    runs = [(flags[0], sums[0])]
    for following in list(zip(flags, sums))[1:]:
        runs.append(combine(runs[-1], following))
    flag, total = runs.pop()

    before = jnp.zeros_like(flag), jnp.zeros_like(total)
    distance = 2 * SQUARE
    while distance < count:
        (got,) = yield [(packed(total, flag, extra), distance)]
        extra = extra + got[part + FLAG :]
        got = got[part : part + 1], got[:part]
        longer = combine(got, before)
        before = [jnp.where(last(distance), new, old) for new, old in zip(longer, before)]
        after, ahead = combine((flag, total), got), combine(got, (flag, total))
        flag, total = (jnp.where(last(distance), b, a) for a, b in zip(after, ahead))
        distance *= 2

    results = [before[1]] + [combine(before, run)[1] for run in runs]
    results = permuted(results, last(2), last(4))
    gots = yield [(results[number], 2 * number) for number in range(1, SQUARE)]
    before = jnp.concatenate([results[0], *gots])
    after = first_core + (1.0 - core_flag) * before
    mine, theirs = crossed(last(1), before, after)
    early(mine)
    (got,) = yield [(theirs, 1)]
    return got, extra


def run(chain, work):
    swaps = next(chain)
    number, done = 0, ()
    while True:
        blocks, _ = lax.optimization_barrier(([block for block, _ in swaps], done))
        done = work[number](blocks[-1]) if number in work else ()
        try:
            swaps = chain.send([swap(b, distance) for b, (_, distance) in zip(blocks, swaps)])
        except StopIteration as end:
            return end.value
        number += 1


def shards(queries, key_vectors, value_vectors, out_grad, norm_gain, doc_bounds):
    tokens, width = queries.shape
    half = width // 2
    pairs = half // E
    rows = pairs * E
    levels = lax.axis_size("ctx").bit_length() - 1
    queries, key_vectors, value_vectors, out_grad, gains, doc_bounds = (
        pltpu.with_memory_space_constraint(x, pltpu.HBM)
        for x in (
            queries, key_vectors, value_vectors, out_grad, norm_gain.reshape(1, width), doc_bounds
        )
    )

    def held(count, columns, dtype=F32, spec=VMEM):
        return spec, jax.ShapeDtypeStruct((count, columns), dtype)

    def call(kernel, inputs, outputs, scratch=(), aliases={}, **sizes):
        return pl.pallas_call(
            functools.partial(kernel, **sizes),
            in_specs=inputs,
            out_specs=[spec for spec, _ in outputs],
            out_shape=[out for _, out in outputs],
            scratch_shapes=scratch,
            input_output_aliases=aliases,
            compiler_params=pltpu.CompilerParams(vmem_limit_bytes=VMEM_LIMIT),
        )

    def copies(*counts):
        return pltpu.SemaphoreType.DMA(counts)

    narrow, single = held(tokens, half, BF16), held(tokens, half)
    grad = held(tokens, width, BF16, ANY)
    row = held(tokens, E, BF16)
    staging = pltpu.VMEM((tokens, half), BF16)
    keys, values, local, carried, middle, spread = {}, {}, {}, {}, {}, {}
    send, keys[1], values[1], start, end, use, tail, flag, bits = call(
        send_state_kernel,
        [ANY] * 3,
        [held(rows + FLAG, E), narrow, narrow, held(tokens, E, jnp.int32),
         held(tokens, E, jnp.int32), row, row, held(FLAG, E), held(FLAG * levels, E)],
        [pltpu.SMEM(doc_bounds.shape, jnp.int32), copies(pairs, 2), copies()],
    )(doc_bounds, key_vectors, value_vectors)
    keep, keys[0], values[0] = call(
        keep_state_kernel,
        [ANY, ANY, VMEM],
        [held(rows, E), narrow, narrow],
        [copies(pairs, 2)],
    )(key_vectors, value_vectors, tail)

    def local_of(other, token):
        local[other] = call(
            local_kernel,
            [ANY] * 3 + [VMEM] * 3 + [ANY],
            [single, narrow, narrow, held(1, width)],
            [copies(pairs, 1), copies(pairs, 1), copies()],
            other=other,
        )(queries, out_grad, gains, keys[other], values[other], start, token)
        return local[other][0]

    def middle_of(other, carry):
        carried[other] = carry
        state = held(rows + FLAG + 2 * pairs, E) if other else held(rows, E)
        middle[other] = call(
            middle_kernel,
            [VMEM] * (8 if other else 6),
            [narrow, state] if other else [narrow, state, held(pairs, E)],
            other=other,
        )(
            *local[other][1:], local[other][0], carry, use,
            *([flag, middle[0][2]] if other else []),
        )

    def spread_of(other, token):
        done = spread[0][:1] if other else []
        spread[other] = call(
            spread_kernel,
            [VMEM] * 8 + [ANY] * (1 + len(done)),
            [grad, single, single],
            [staging, copies(pairs)],
            {9: 0} if done else {},
            other=other,
        )(
            local[other][1], keys[other], values[other], middle[other][0], carried[other],
            use, start, end, token, *done,
        )
        return spread[other][1]

    grads = []

    def final_of(other, later):
        grads[:] = call(
            final_kernel,
            [VMEM] * 6 + [ANY] * len(grads),
            [grad, grad],
            [staging, staging, copies(pairs, 2)],
            {6: 0, 7: 1} if grads else {},
            other=other,
        )(keys[other], values[other], *spread[other][1:], later, tail, *grads)

    def chain():
        got, _ = yield from scan(keep, send, bits, False, functools.partial(middle_of, 0))
        middle_of(1, got)
        states = middle[0][1], middle[1][1]
        got, total = yield from scan(*states, bits, True, functools.partial(final_of, 0))
        final_of(1, got)
        return total

    steps = levels + 1
    work = {}
    for begin, part in ((0, local_of), (steps, spread_of)):
        work[begin + 1] = functools.partial(part, 0)
        work[begin + steps - 3] = functools.partial(part, 1)
    total = run(chain(), work)
    gain_grad = total.reshape(width) / math.sqrt(tokens * lax.axis_size("ctx"))
    return spread[1][0], *grads, gain_grad


def solution(mesh):
    tokens = P(("parts", "ctx"), None)
    return jax.shard_map(
        shards,
        mesh=mesh,
        in_specs=(tokens, tokens, tokens, tokens, P(), P(None, ("parts", "ctx"))),
        out_specs=(tokens, tokens, tokens, P("parts")),
        check_vma=False,
    )
```

```python
import functools
import math

import jax
import jax.numpy as jnp
from jax import lax
from jax.experimental import pallas as pl
from jax.experimental.pallas import tpu as pltpu
from jax.sharding import PartitionSpec as P

E = 128
PAIR = 2 * E
FLAG = 8
SQUARE = 4
TOGETHER = 8
EPS = 1e-06
VMEM_LIMIT = 8 * 1024 * 1024
F32 = jnp.float32
BF16 = jnp.bfloat16
VMEM = pl.BlockSpec(memory_space=pltpu.VMEM)
ANY = pl.BlockSpec(memory_space=pl.ANY)


def dot(a, b, a_dim, b_dim):
    return lax.dot_general(a, b, (((a_dim,), (b_dim,)), ((), ())), preferred_element_type=F32)


def head(h):
    return slice(h * E, (h + 1) * E)


def place(pair, pairs):
    chip = (lax.axis_index("ctx") // 2) % SQUARE
    slot = ((pair % SQUARE) ^ chip) * (pairs // SQUARE) + pair // SQUARE
    return pl.ds(pl.multiple_of(slot * E, E), E)


def owner_column(pair, other):
    core = lax.axis_index("ctx") % 2
    return pl.ds(pl.multiple_of((2 * pair + (core + other) % 2) * E, E), E)


def fetch(other, sources, targets, sems):
    copies = []
    for pair in range(targets[0].shape[1] // E):
        copies.append([])
        for i, (source, target) in enumerate(zip(sources, targets)):
            copy = pltpu.make_async_copy(
                source.at[:, owner_column(pair, other)], target.at[:, head(pair)], sems.at[pair, i]
            )
            copy.start()
            copies[-1].append(copy)
    return copies


def put(source, target, pair, other, sem):
    copy = pltpu.make_async_copy(
        source.at[:, head(pair)], target.at[:, owner_column(pair, other)], sem
    )
    copy.start()
    return copy


def row_values(values, rows, dtype):
    position = lax.broadcasted_iota(jnp.int32, (rows, E), 0)
    result = jnp.full((rows, E), values[0])
    for block in range(1, len(values)):
        result = jnp.where(position >= block * (rows // len(values)), values[block], result)
    return result.astype(dtype)


def states_of(k_ref, v_ref, tail_ref, copies, out_ref):
    pairs = len(copies)
    for begin in range(0, pairs, TOGETHER):
        together = range(begin, min(begin + TOGETHER, pairs))
        for pair in together:
            for copy in copies[pair]:
                copy.wait()
        for pair in together:
            state = dot(k_ref[:, head(pair)] * tail_ref[...], v_ref[:, head(pair)], 0, 0)
            out_ref[place(pair, pairs), :] = state


def send_state_kernel(
    bounds_hbm, k_hbm, v_hbm,
    send_ref, k_ref, v_ref, start_ref, end_ref, use_ref, tail_ref, flag_ref, bits_ref,
    bounds, sems, bounds_sem,
):
    bounds_copy = pltpu.make_async_copy(bounds_hbm, bounds, bounds_sem)
    bounds_copy.start()
    copies = fetch(1, (k_hbm, v_hbm), (k_ref, v_ref), sems)
    rows, width = k_ref.shape
    count = bounds.shape[1]
    block_len = rows // count
    me = lax.axis_index("ctx")
    first = me * count
    for bit in range(bits_ref.shape[0] // FLAG):
        value = jnp.full((FLAG, E), (me // 2**bit) % 2)
        bits_ref[bit * FLAG : (bit + 1) * FLAG, :] = value.astype(F32)
    bounds_copy.wait()
    opens = [bounds[0, b] for b in range(count)]
    closes = [bounds[1, b] for b in range(count)]
    flag = jnp.full((FLAG, E), (opens[-1] >= first).astype(F32))
    flag_ref[...] = flag
    send_ref[width:, :] = flag
    use_ref[...] = row_values([(x < first).astype(F32) for x in opens], rows, BF16)
    tail_ref[...] = row_values([(x >= first + count - 1).astype(F32) for x in closes], rows, BF16)
    start_ref[...] = row_values([(x - first) * block_len for x in opens], rows, jnp.int32)
    end_ref[...] = row_values([(x - first + 1) * block_len for x in closes], rows, jnp.int32)
    states_of(k_ref, v_ref, tail_ref, copies, send_ref)


def keep_state_kernel(k_hbm, v_hbm, tail_ref, keep_ref, k_ref, v_ref, sems):
    copies = fetch(0, (k_hbm, v_hbm), (k_ref, v_ref), sems)
    states_of(k_ref, v_ref, tail_ref, copies, keep_ref)


def sight(bound_ref, turned):
    rows = bound_ref.shape[0]
    row = lax.broadcasted_iota(jnp.int32, (rows, E), 0)
    parts = []
    for c in range(rows // E):
        column = lax.broadcasted_iota(jnp.int32, (rows, E), 1) + c * E
        if turned:
            seen = (column >= row) & (column < bound_ref[...])
        else:
            seen = (column <= row) & (column >= bound_ref[...])
        parts.append(jnp.where(seen, 1.0, 0.0).astype(BF16))
    return jnp.concatenate(parts, axis=1)


def local_kernel(
    q_hbm, g_hbm, gain_hbm, k_ref, v_ref, start_ref, _,
    out_ref, q_ref, g_ref, gain_ref, q_sems, g_sems, gain_sem, *, other,
):
    copies = fetch(other, [q_hbm], [q_ref], q_sems)
    grad_copies = fetch(other, [g_hbm], [g_ref], g_sems)
    gain_copy = pltpu.make_async_copy(gain_hbm, gain_ref, gain_sem)
    gain_copy.start()
    mask = sight(start_ref, False)
    pairs = len(copies)
    for begin in range(0, pairs, TOGETHER):
        together = range(begin, min(begin + TOGETHER, pairs))
        for pair in together:
            copies[pair][0].wait()
        for pair in together:
            c = head(pair)
            scores = dot(q_ref[:, c], k_ref[:, c], 1, 1).astype(BF16) * mask
            out_ref[:, c] = dot(scores, v_ref[:, c], 1, 0)
    for (copy,) in grad_copies:
        copy.wait()
    gain_copy.wait()


def middle_kernel(q_ref, g_ref, gain_ref, local_ref, carry_ref, use_ref, *rest, other):
    if other:
        flag_ref, sums_ref, d_ref, state_ref = rest
    else:
        d_ref, state_ref, sums_ref = rest
    pairs = q_ref.shape[1] // E
    use = use_ref[...]
    core = lax.axis_index("ctx") % 2
    for pair in range(pairs):
        c = head(pair)
        used = q_ref[:, c] * use
        carry = carry_ref[place(pair, pairs), :].astype(BF16)
        attended = local_ref[:, c] + dot(used, carry, 1, 0)
        grad = g_ref[:, c].astype(F32)
        d_norm = grad * gain_ref[:, owner_column(pair, other)]
        square = jnp.mean(attended * attended, axis=1, keepdims=True)
        centre = jnp.mean(d_norm * attended, axis=1, keepdims=True)
        inverse = lax.rsqrt(square + EPS)
        gained = grad * (attended * inverse)
        d_att = ((d_norm - attended * (centre * inverse * inverse)) * inverse).astype(BF16)
        d_ref[:, c] = d_att
        state_ref[place(pair, pairs), :] = dot(used, d_att, 0, 0)
        total = jnp.sum(gained, axis=0, keepdims=True)
        if other:
            both = jnp.concatenate(
                crossed(core == 0, total, sums_ref[pair : pair + 1, :])
            )
            begin = pairs * E + FLAG + 2 * pair
            state_ref[begin : begin + 2, :] = both
        else:
            sums_ref[pair : pair + 1, :] = total
    if other:
        state_ref[pairs * E : pairs * E + FLAG, :] = flag_ref[...]


def spread_kernel(
    q_ref, k_ref, v_ref, d_ref, carry_ref, use_ref, start_ref, end_ref, *rest, other
):
    qg_hbm, kp_ref, vp_ref, qg_ref, sems = rest[-5:]
    pairs = q_ref.shape[1] // E
    use = use_ref[...]
    mask = sight(start_ref, False)
    turned_mask = sight(end_ref, True)
    copies = []
    for pair in range(pairs):
        c = head(pair)
        carry = carry_ref[place(pair, pairs), :].astype(BF16)
        query, key, value, d_att = q_ref[:, c], k_ref[:, c], v_ref[:, c], d_ref[:, c]
        dscores = dot(d_att, value, 1, 1).astype(BF16) * mask
        from_carry = dot(d_att * use, carry, 1, 1)
        qg_ref[:, c] = (dot(dscores, key, 1, 0) + from_carry).astype(BF16)
        turned = dot(value, d_att, 1, 1).astype(BF16) * turned_mask
        kp_ref[:, c] = dot(turned, query, 1, 0)
        turned = dot(key, query, 1, 1).astype(BF16) * turned_mask
        vp_ref[:, c] = dot(turned, d_att, 1, 0)
        copies.append(put(qg_ref, qg_hbm, pair, other, sems.at[pair]))
    for copy in copies:
        copy.wait()


def final_kernel(k_ref, v_ref, kp_ref, vp_ref, later_ref, tail_ref, *rest, other):
    kg_hbm, vg_hbm, kg_ref, vg_ref, sems = rest[-5:]
    pairs = k_ref.shape[1] // E
    tail = tail_ref[...]
    copies = []
    for pair in range(pairs):
        c = head(pair)
        later = later_ref[place(pair, pairs), :].astype(BF16)
        kg_ref[:, c] = (kp_ref[:, c] + dot(v_ref[:, c] * tail, later, 1, 1)).astype(BF16)
        vg_ref[:, c] = (vp_ref[:, c] + dot(k_ref[:, c] * tail, later, 1, 0)).astype(BF16)
        copies.append(put(kg_ref, kg_hbm, pair, other, sems.at[pair, 0]))
        copies.append(put(vg_ref, vg_hbm, pair, other, sems.at[pair, 1]))
    for copy in copies:
        copy.wait()


def swap(block, distance):
    count = lax.axis_size("ctx")
    return lax.ppermute(block, "ctx", [(i, i ^ distance) for i in range(count)])


def combine(early, late):
    return jnp.maximum(early[0], late[0]), late[1] + (1.0 - late[0]) * early[1]


def crossed(bit, zero, one):
    return jnp.where(bit, one, zero), jnp.where(bit, zero, one)


def permuted(parts, low, high):
    a, b = crossed(low, parts[0], parts[1])
    c, d = crossed(low, parts[2], parts[3])
    a, c = crossed(high, a, c)
    b, d = crossed(high, b, d)
    return [a, b, c, d]


def scan(keep, send, bits, backward, early):
    count = lax.axis_size("ctx")
    rows = keep.shape[0]
    part = rows // SQUARE

    def last(distance):
        row = FLAG * (distance.bit_length() - 1)
        bit = bits[row : row + 1]
        return bit < 0.5 if backward else bit > 0.5

    def packed(block, flag, extra):
        return jnp.concatenate([block, jnp.broadcast_to(flag, (FLAG, E)), extra])

    (got,) = yield [(send, 1)]
    core_flag, late_flag = crossed(last(1), send[rows : rows + 1], got[rows : rows + 1])
    extra = send[rows + FLAG :] + got[rows + FLAG :]
    first_core = jnp.where(last(1), got[:rows], keep)
    flag = jnp.maximum(core_flag, late_flag)

    def both_cores(number):
        where = slice(number * part, (number + 1) * part)
        early, late = crossed(last(1), keep[where], got[where])
        return late + (1.0 - late_flag) * early

    gots = yield [
        (packed(both_cores(number), flag, extra), 2 * number) for number in range(1, SQUARE)
    ]
    extra = sum((got[part + FLAG :] for got in gots), extra)
    flags = permuted([flag] + [got[part : part + 1] for got in gots], last(2), last(4))
    sums = permuted([both_cores(0)] + [got[:part] for got in gots], last(2), last(4))
    runs = [(flags[0], sums[0])]
    for following in list(zip(flags, sums))[1:]:
        runs.append(combine(runs[-1], following))
    flag, total = runs.pop()

    before = jnp.zeros_like(flag), jnp.zeros_like(total)
    distance = 2 * SQUARE
    while distance < count:
        (got,) = yield [(packed(total, flag, extra), distance)]
        extra = extra + got[part + FLAG :]
        got = got[part : part + 1], got[:part]
        longer = combine(got, before)
        before = [jnp.where(last(distance), new, old) for new, old in zip(longer, before)]
        after, ahead = combine((flag, total), got), combine(got, (flag, total))
        flag, total = (jnp.where(last(distance), b, a) for a, b in zip(after, ahead))
        distance *= 2

    results = [before[1]] + [combine(before, run)[1] for run in runs]
    results = permuted(results, last(2), last(4))
    gots = yield [(results[number], 2 * number) for number in range(1, SQUARE)]
    before = jnp.concatenate([results[0], *gots])
    after = first_core + (1.0 - core_flag) * before
    mine, theirs = crossed(last(1), before, after)
    early(mine)
    (got,) = yield [(theirs, 1)]
    return got, extra


def run(chain, work):
    swaps = next(chain)
    number, done = 0, ()
    while True:
        blocks, _ = lax.optimization_barrier(([block for block, _ in swaps], done))
        done = work[number](blocks[-1]) if number in work else ()
        try:
            swaps = chain.send([swap(b, distance) for b, (_, distance) in zip(blocks, swaps)])
        except StopIteration as end:
            return end.value
        number += 1


def shards(queries, key_vectors, value_vectors, out_grad, norm_gain, doc_bounds):
    tokens, width = queries.shape
    half = width // 2
    pairs = half // E
    rows = pairs * E
    levels = lax.axis_size("ctx").bit_length() - 1
    queries, key_vectors, value_vectors, out_grad, gains, doc_bounds = (
        pltpu.with_memory_space_constraint(x, pltpu.HBM)
        for x in (
            queries, key_vectors, value_vectors, out_grad, norm_gain.reshape(1, width), doc_bounds
        )
    )

    def held(count, columns, dtype=F32, spec=VMEM):
        return spec, jax.ShapeDtypeStruct((count, columns), dtype)

    def call(kernel, inputs, outputs, scratch=(), aliases={}, **sizes):
        return pl.pallas_call(
            functools.partial(kernel, **sizes),
            in_specs=inputs,
            out_specs=[spec for spec, _ in outputs],
            out_shape=[out for _, out in outputs],
            scratch_shapes=scratch,
            input_output_aliases=aliases,
            compiler_params=pltpu.CompilerParams(vmem_limit_bytes=VMEM_LIMIT),
        )

    def copies(*counts):
        return pltpu.SemaphoreType.DMA(counts)

    narrow, single = held(tokens, half, BF16), held(tokens, half)
    grad = held(tokens, width, BF16, ANY)
    row = held(tokens, E, BF16)
    staging = pltpu.VMEM((tokens, half), BF16)
    keys, values, local, carried, middle, spread = {}, {}, {}, {}, {}, {}
    send, keys[1], values[1], start, end, use, tail, flag, bits = call(
        send_state_kernel,
        [ANY] * 3,
        [held(rows + FLAG, E), narrow, narrow, held(tokens, E, jnp.int32),
         held(tokens, E, jnp.int32), row, row, held(FLAG, E), held(FLAG * levels, E)],
        [pltpu.SMEM(doc_bounds.shape, jnp.int32), copies(pairs, 2), copies()],
    )(doc_bounds, key_vectors, value_vectors)
    keep, keys[0], values[0] = call(
        keep_state_kernel,
        [ANY, ANY, VMEM],
        [held(rows, E), narrow, narrow],
        [copies(pairs, 2)],
    )(key_vectors, value_vectors, tail)

    def local_of(other, token):
        local[other] = call(
            local_kernel,
            [ANY] * 3 + [VMEM] * 3 + [ANY],
            [single, narrow, narrow, held(1, width)],
            [copies(pairs, 1), copies(pairs, 1), copies()],
            other=other,
        )(queries, out_grad, gains, keys[other], values[other], start, token)
        return local[other][0]

    def middle_of(other, carry):
        carried[other] = carry
        state = held(rows + FLAG + 2 * pairs, E) if other else held(rows, E)
        middle[other] = call(
            middle_kernel,
            [VMEM] * (8 if other else 6),
            [narrow, state] if other else [narrow, state, held(pairs, E)],
            other=other,
        )(
            *local[other][1:], local[other][0], carry, use,
            *([flag, middle[0][2]] if other else []),
        )

    def spread_of(other, token):
        done = spread[0][:1] if other else []
        spread[other] = call(
            spread_kernel,
            [VMEM] * 8 + [ANY] * (1 + len(done)),
            [grad, single, single],
            [staging, copies(pairs)],
            {9: 0} if done else {},
            other=other,
        )(
            local[other][1], keys[other], values[other], middle[other][0], carried[other],
            use, start, end, token, *done,
        )
        return spread[other][1]

    grads = []

    def final_of(other, later):
        grads[:] = call(
            final_kernel,
            [VMEM] * 6 + [ANY] * len(grads),
            [grad, grad],
            [staging, staging, copies(pairs, 2)],
            {6: 0, 7: 1} if grads else {},
            other=other,
        )(keys[other], values[other], *spread[other][1:], later, tail, *grads)

    def chain():
        got, _ = yield from scan(keep, send, bits, False, functools.partial(middle_of, 0))
        middle_of(1, got)
        states = middle[0][1], middle[1][1]
        got, total = yield from scan(*states, bits, True, functools.partial(final_of, 0))
        final_of(1, got)
        return total

    steps = levels + 1
    work = {}
    for begin, part in ((0, local_of), (steps, spread_of)):
        work[begin + 1] = functools.partial(part, 0)
        work[begin + steps - 3] = functools.partial(part, 1)
    total = run(chain(), work)
    gain_grad = total.reshape(width) / math.sqrt(tokens * lax.axis_size("ctx"))
    return spread[1][0], *grads, gain_grad


def solution(mesh):
    tokens = P(("parts", "ctx"), None)
    return jax.shard_map(
        shards,
        mesh=mesh,
        in_specs=(tokens, tokens, tokens, tokens, P(), P(None, ("parts", "ctx"))),
        out_specs=(tokens, tokens, tokens, P("parts")),
        check_vma=False,
    )
```

```python
import functools
import math

import jax
import jax.numpy as jnp
from jax import lax
from jax.experimental import pallas as pl
from jax.experimental.pallas import tpu as pltpu
from jax.sharding import PartitionSpec as P

E = 128
PAIR = 2 * E
FLAG = 8
SQUARE = 4
TOGETHER = 8
EPS = 1e-06
VMEM_LIMIT = 8 * 1024 * 1024
F32 = jnp.float32
BF16 = jnp.bfloat16
VMEM = pl.BlockSpec(memory_space=pltpu.VMEM)
ANY = pl.BlockSpec(memory_space=pl.ANY)


def dot(a, b, a_dim, b_dim):
    return lax.dot_general(a, b, (((a_dim,), (b_dim,)), ((), ())), preferred_element_type=F32)


def head(h):
    return slice(h * E, (h + 1) * E)


def place(pair, pairs):
    chip = (lax.axis_index("ctx") // 2) % SQUARE
    slot = ((pair % SQUARE) ^ chip) * (pairs // SQUARE) + pair // SQUARE
    return pl.ds(pl.multiple_of(slot * E, E), E)


def owner_column(pair, other):
    core = lax.axis_index("ctx") % 2
    return pl.ds(pl.multiple_of((2 * pair + (core + other) % 2) * E, E), E)


def fetch(other, sources, targets, sems):
    copies = []
    for pair in range(targets[0].shape[1] // E):
        copies.append([])
        for i, (source, target) in enumerate(zip(sources, targets)):
            copy = pltpu.make_async_copy(
                source.at[:, owner_column(pair, other)], target.at[:, head(pair)], sems.at[pair, i]
            )
            copy.start()
            copies[-1].append(copy)
    return copies


def put(source, target, pair, other, sem):
    copy = pltpu.make_async_copy(
        source.at[:, head(pair)], target.at[:, owner_column(pair, other)], sem
    )
    copy.start()
    return copy


def row_values(values, rows, dtype):
    position = lax.broadcasted_iota(jnp.int32, (rows, E), 0)
    result = jnp.full((rows, E), values[0])
    for block in range(1, len(values)):
        result = jnp.where(position >= block * (rows // len(values)), values[block], result)
    return result.astype(dtype)


def states_of(k_ref, v_ref, tail_ref, copies, out_ref):
    pairs = len(copies)
    for begin in range(0, pairs, TOGETHER):
        together = range(begin, min(begin + TOGETHER, pairs))
        for pair in together:
            for copy in copies[pair]:
                copy.wait()
        for pair in together:
            state = dot(k_ref[:, head(pair)] * tail_ref[...], v_ref[:, head(pair)], 0, 0)
            out_ref[place(pair, pairs), :] = state


def send_state_kernel(
    bounds_hbm, k_hbm, v_hbm,
    send_ref, k_ref, v_ref, start_ref, end_ref, use_ref, tail_ref, flag_ref, bits_ref,
    bounds, sems, bounds_sem,
):
    bounds_copy = pltpu.make_async_copy(bounds_hbm, bounds, bounds_sem)
    bounds_copy.start()
    copies = fetch(1, (k_hbm, v_hbm), (k_ref, v_ref), sems)
    rows, width = k_ref.shape
    count = bounds.shape[1]
    block_len = rows // count
    me = lax.axis_index("ctx")
    first = me * count
    for bit in range(bits_ref.shape[0] // FLAG):
        value = jnp.full((FLAG, E), (me // 2**bit) % 2)
        bits_ref[bit * FLAG : (bit + 1) * FLAG, :] = value.astype(F32)
    bounds_copy.wait()
    opens = [bounds[0, b] for b in range(count)]
    closes = [bounds[1, b] for b in range(count)]
    flag = jnp.full((FLAG, E), (opens[-1] >= first).astype(F32))
    flag_ref[...] = flag
    send_ref[width:, :] = flag
    use_ref[...] = row_values([(x < first).astype(F32) for x in opens], rows, BF16)
    tail_ref[...] = row_values([(x >= first + count - 1).astype(F32) for x in closes], rows, BF16)
    start_ref[...] = row_values([(x - first) * block_len for x in opens], rows, jnp.int32)
    end_ref[...] = row_values([(x - first + 1) * block_len for x in closes], rows, jnp.int32)
    states_of(k_ref, v_ref, tail_ref, copies, send_ref)


def keep_state_kernel(k_hbm, v_hbm, tail_ref, keep_ref, k_ref, v_ref, sems):
    copies = fetch(0, (k_hbm, v_hbm), (k_ref, v_ref), sems)
    states_of(k_ref, v_ref, tail_ref, copies, keep_ref)


def sight(bound_ref, turned):
    rows = bound_ref.shape[0]
    row = lax.broadcasted_iota(jnp.int32, (rows, E), 0)
    parts = []
    for c in range(rows // E):
        column = lax.broadcasted_iota(jnp.int32, (rows, E), 1) + c * E
        if turned:
            seen = (column >= row) & (column < bound_ref[...])
        else:
            seen = (column <= row) & (column >= bound_ref[...])
        parts.append(jnp.where(seen, 1.0, 0.0).astype(BF16))
    return jnp.concatenate(parts, axis=1)


def attend(q_ref, k_ref, v_ref, copies, mask, put_out):
    pairs = len(copies)
    for begin in range(0, pairs, TOGETHER):
        together = range(begin, min(begin + TOGETHER, pairs))
        for pair in together:
            copies[pair][0].wait()
        for pair in together:
            c = head(pair)
            scores = dot(q_ref[:, c], k_ref[:, c], 1, 1).astype(BF16) * mask
            put_out(c, dot(scores, v_ref[:, c], 1, 0))


def local_kernel(
    q_hbm, g_hbm, gain_hbm, k_ref, v_ref, start_ref, _,
    out_ref, q_ref, g_ref, gain_ref, q_sems, g_sems, gain_sem,
):
    copies = fetch(0, [q_hbm], [q_ref], q_sems)
    grad_copies = fetch(0, [g_hbm], [g_ref], g_sems)
    gain_copy = pltpu.make_async_copy(gain_hbm, gain_ref, gain_sem)
    gain_copy.start()

    def put_out(c, local):
        out_ref[:, c] = local

    attend(q_ref, k_ref, v_ref, copies, sight(start_ref, False), put_out)
    for (copy,) in grad_copies:
        copy.wait()
    gain_copy.wait()


def other_local_kernel(
    q_hbm, g_hbm, k_ref, v_ref, start_ref, use_ref, _,
    out_ref, q_ref, g_ref, q_sems, g_sems,
):
    copies = fetch(1, [q_hbm], [q_ref], q_sems)
    grad_copies = fetch(1, [g_hbm], [g_ref], g_sems)
    rows = q_ref.shape[0]
    use = use_ref[...]

    def put_out(c, local):
        out_ref[:rows, c] = local
        out_ref[rows : 2 * rows, c] = (q_ref[:, c] * use).astype(F32)

    attend(q_ref, k_ref, v_ref, copies, sight(start_ref, False), put_out)
    for (copy,) in grad_copies:
        copy.wait()
    for pair in range(len(copies)):
        out_ref[2 * rows :, head(pair)] = g_ref[:, head(pair)].astype(F32)


def through_norm(local, used, grad, gain, carry):
    attended = local + dot(used, carry.astype(BF16), 1, 0)
    d_norm = grad * gain
    square = jnp.mean(attended * attended, axis=1, keepdims=True)
    centre = jnp.mean(d_norm * attended, axis=1, keepdims=True)
    inverse = lax.rsqrt(square + EPS)
    total = jnp.sum(grad * (attended * inverse), axis=0, keepdims=True)
    d_att = ((d_norm - attended * (centre * inverse * inverse)) * inverse).astype(BF16)
    return d_att, dot(used, d_att, 0, 0), total


def middle_kernel(
    q_ref, g_ref, gain_ref, local_ref, other_ref, mine_ref, theirs_ref, use_ref,
    d_ref, other_d_ref, state_ref, other_state_ref, sums_ref,
):
    rows = q_ref.shape[0]
    pairs = q_ref.shape[1] // E
    for pair in range(pairs):
        c, where = head(pair), place(pair, pairs)
        gain = gain_ref[:, owner_column(pair, 0)]
        d_att, state, total = through_norm(
            local_ref[:, c], q_ref[:, c] * use_ref[...], g_ref[:, c].astype(F32), gain,
            mine_ref[where, :],
        )
        d_ref[:, c] = d_att
        state_ref[where, :] = state
        d_att, state, other_total = through_norm(
            other_ref[:rows, c], other_ref[rows : 2 * rows, c].astype(BF16),
            other_ref[2 * rows :, c], gain, theirs_ref[where, :],
        )
        other_d_ref[:, c] = d_att.astype(F32)
        other_state_ref[where, :] = state
        sums_ref[pair : pair + 1, :] = total + other_total


def spread_kernel(
    q_ref, k_ref, v_ref, d_ref, carry_ref, use_ref, start_ref, end_ref, *rest, other
):
    qg_hbm, kp_ref, vp_ref, qg_ref, sems = rest[-5:]
    pairs = q_ref.shape[1] // E
    use = use_ref[...]
    mask = sight(start_ref, False)
    turned_mask = sight(end_ref, True)
    copies = []
    for pair in range(pairs):
        c = head(pair)
        carry = carry_ref[place(pair, pairs), :].astype(BF16)
        query, key, value, d_att = q_ref[:, c], k_ref[:, c], v_ref[:, c], d_ref[:, c].astype(BF16)
        dscores = dot(d_att, value, 1, 1).astype(BF16) * mask
        from_carry = dot(d_att * use, carry, 1, 1)
        qg_ref[:, c] = (dot(dscores, key, 1, 0) + from_carry).astype(BF16)
        turned = dot(value, d_att, 1, 1).astype(BF16) * turned_mask
        kp_ref[:, c] = dot(turned, query, 1, 0)
        turned = dot(key, query, 1, 1).astype(BF16) * turned_mask
        vp_ref[:, c] = dot(turned, d_att, 1, 0)
        copies.append(put(qg_ref, qg_hbm, pair, other, sems.at[pair]))
    for copy in copies:
        copy.wait()


def final_kernel(k_ref, v_ref, kp_ref, vp_ref, later_ref, tail_ref, *rest, other):
    kg_hbm, vg_hbm, kg_ref, vg_ref, sems = rest[-5:]
    pairs = k_ref.shape[1] // E
    tail = tail_ref[...]
    copies = []
    for pair in range(pairs):
        c = head(pair)
        later = later_ref[place(pair, pairs), :].astype(BF16)
        kg_ref[:, c] = (kp_ref[:, c] + dot(v_ref[:, c] * tail, later, 1, 1)).astype(BF16)
        vg_ref[:, c] = (vp_ref[:, c] + dot(k_ref[:, c] * tail, later, 1, 0)).astype(BF16)
        copies.append(put(kg_ref, kg_hbm, pair, other, sems.at[pair, 0]))
        copies.append(put(vg_ref, vg_hbm, pair, other, sems.at[pair, 1]))
    for copy in copies:
        copy.wait()


def swap(block, distance):
    count = lax.axis_size("ctx")
    return lax.ppermute(block, "ctx", [(i, i ^ distance) for i in range(count)])


def combine(early, late):
    return jnp.maximum(early[0], late[0]), late[1] + (1.0 - late[0]) * early[1]


def crossed(bit, zero, one):
    return jnp.where(bit, one, zero), jnp.where(bit, zero, one)


def permuted(parts, low, high):
    a, b = crossed(low, parts[0], parts[1])
    c, d = crossed(low, parts[2], parts[3])
    a, c = crossed(high, a, c)
    b, d = crossed(high, b, d)
    return [a, b, c, d]


def scan(own, partner, own_flag, partner_flag, extra, bits, backward, summed):
    count = lax.axis_size("ctx")
    rows = own.shape[0]
    part = rows // SQUARE

    def last(distance):
        row = FLAG * (distance.bit_length() - 1)
        bit = bits[row : row + 1]
        return bit < 0.5 if backward else bit > 0.5

    def packed(block, flag, extra):
        return jnp.concatenate([block, jnp.broadcast_to(flag, (FLAG, E)), extra])

    core_flag, late_flag = crossed(last(1), own_flag, partner_flag)
    first_core = jnp.where(last(1), partner, own)
    flag = jnp.maximum(core_flag, late_flag)

    def both_cores(number):
        where = slice(number * part, (number + 1) * part)
        early, late = crossed(last(1), own[where], partner[where])
        return late + (1.0 - late_flag) * early

    gots = yield [
        (packed(both_cores(number), flag, extra), 2 * number) for number in range(1, SQUARE)
    ]
    extra = sum((got[part + FLAG :] for got in gots), extra)
    flags = permuted([flag] + [got[part : part + 1] for got in gots], last(2), last(4))
    sums = permuted([both_cores(0)] + [got[:part] for got in gots], last(2), last(4))
    runs = [(flags[0], sums[0])]
    for following in list(zip(flags, sums))[1:]:
        runs.append(combine(runs[-1], following))
    flag, total = runs.pop()

    before = jnp.zeros_like(flag), jnp.zeros_like(total)
    distance = 2 * SQUARE
    while distance < count:
        (got,) = yield [(packed(total, flag, extra), distance)]
        extra = extra + got[part + FLAG :]
        got = got[part : part + 1], got[:part]
        longer = combine(got, before)
        before = [jnp.where(last(distance), new, old) for new, old in zip(longer, before)]
        after, ahead = combine((flag, total), got), combine(got, (flag, total))
        flag, total = (jnp.where(last(distance), b, a) for a, b in zip(after, ahead))
        distance *= 2

    summed(extra)
    results = [before[1]] + [combine(before, run)[1] for run in runs]
    results = permuted(results, last(2), last(4))
    gots = yield [(results[number], 2 * number) for number in range(1, SQUARE)]
    before = jnp.concatenate([results[0], *gots])
    after = first_core + (1.0 - core_flag) * before
    return crossed(last(1), before, after)


def run(chain, work):
    swaps = next(chain)
    number, done = 0, ()
    while True:
        blocks, _ = lax.optimization_barrier(([block for block, _ in swaps], done))
        done = work[number](blocks[-1]) if number in work else ()
        try:
            swaps = chain.send([swap(b, distance) for b, (_, distance) in zip(blocks, swaps)])
        except StopIteration as end:
            return end.value
        number += 1


def shards(queries, key_vectors, value_vectors, out_grad, norm_gain, doc_bounds):
    tokens, width = queries.shape
    half = width // 2
    pairs = half // E
    rows = pairs * E
    levels = lax.axis_size("ctx").bit_length() - 1
    queries, key_vectors, value_vectors, out_grad, gains, doc_bounds = (
        pltpu.with_memory_space_constraint(x, pltpu.HBM)
        for x in (
            queries, key_vectors, value_vectors, out_grad, norm_gain.reshape(1, width), doc_bounds
        )
    )

    def held(count, columns, dtype=F32, spec=VMEM):
        return spec, jax.ShapeDtypeStruct((count, columns), dtype)

    def call(kernel, inputs, outputs, scratch=(), aliases={}, **sizes):
        return pl.pallas_call(
            functools.partial(kernel, **sizes),
            in_specs=inputs,
            out_specs=[spec for spec, _ in outputs],
            out_shape=[out for _, out in outputs],
            scratch_shapes=scratch,
            input_output_aliases=aliases,
            compiler_params=pltpu.CompilerParams(vmem_limit_bytes=VMEM_LIMIT),
        )

    def copies(*counts):
        return pltpu.SemaphoreType.DMA(counts)

    narrow, single = held(tokens, half, BF16), held(tokens, half)
    grad = held(tokens, width, BF16, ANY)
    row = held(tokens, E, BF16)
    staging = pltpu.VMEM((tokens, half), BF16)
    keys, values, query, local, carried, d_att, spread = {}, {}, {}, {}, {}, {}, {}
    norm_inputs, middle = [], []
    send, keys[1], values[1], start, end, use, tail, flag, bits = call(
        send_state_kernel,
        [ANY] * 3,
        [held(rows + FLAG, E), narrow, narrow, held(tokens, E, jnp.int32),
         held(tokens, E, jnp.int32), row, row, held(FLAG, E), held(FLAG * levels, E)],
        [pltpu.SMEM(doc_bounds.shape, jnp.int32), copies(pairs, 2), copies()],
    )(doc_bounds, key_vectors, value_vectors)
    keep, keys[0], values[0] = call(
        keep_state_kernel,
        [ANY, ANY, VMEM],
        [held(rows, E), narrow, narrow],
        [copies(pairs, 2)],
    )(key_vectors, value_vectors, tail)

    def other_local_of(token):
        pack, other_query = call(
            other_local_kernel,
            [ANY] * 2 + [VMEM] * 4 + [ANY],
            [held(3 * tokens, half), narrow],
            [pltpu.VMEM((tokens, half), BF16), copies(pairs, 1), copies(pairs, 1)],
        )(queries, out_grad, keys[1], values[1], start, use, token)
        query[1] = other_query
        middle[:] = [pack]
        return other_query

    def local_of(token):
        local[0], query[0], *rest = call(
            local_kernel,
            [ANY] * 3 + [VMEM] * 3 + [ANY],
            [single, narrow, narrow, held(1, width)],
            [copies(pairs, 1), copies(pairs, 1), copies()],
        )(queries, out_grad, gains, keys[0], values[0], start, token)
        norm_inputs[:] = rest
        local[1] = swap(lax.optimization_barrier((middle[0], token))[0], 1)
        return local[0], local[1]

    def spread_of(other, token):
        done = spread[0][:1] if other else []
        spread[other] = call(
            spread_kernel,
            [VMEM] * 8 + [ANY] * (1 + len(done)),
            [grad, single, single],
            [staging, copies(pairs)],
            {9: 0} if done else {},
            other=other,
        )(
            query[other], keys[other], values[other], d_att[other], carried[other],
            use, start, end, token, *done,
        )
        return spread[other][1]

    def first_spread_of(token):
        done = spread_of(0, token)
        d_other, theirs = lax.optimization_barrier((middle, done))[0]
        d_att[1], carried[1] = swap(d_other, 1), swap(theirs, 1)
        return done

    def last_spread_of(token):
        done = spread_of(1, token)
        sums = lax.optimization_barrier((gain_sums[0], done))[0]
        gain_sums.append(swap(sums, 1))
        return done, gain_sums[1]

    grads, gain_sums = [], []

    def final_of(other, later):
        grads[:] = call(
            final_kernel,
            [VMEM] * 6 + [ANY] * len(grads),
            [grad, grad],
            [staging, staging, copies(pairs, 2)],
            {6: 0, 7: 1} if grads else {},
            other=other,
        )(keys[other], values[other], *spread[other][1:], later, tail, *grads)

    def chain():
        (got,) = yield [(send, 1)]
        own_flag, other_flag = flag[:1], got[rows : rows + 1]
        nothing = jnp.zeros((0, E), F32)
        mine, theirs = yield from scan(
            keep, got[:rows], own_flag, other_flag, nothing, bits, False, lambda _: None
        )
        carried[0] = mine
        d_att[0], other_d, state, other_state, sums = call(
            middle_kernel,
            [VMEM] * 8,
            [narrow, single, held(rows, E), held(rows, E), held(pairs, E)],
        )(query[0], *norm_inputs, local[0], local[1], mine, theirs, use)
        middle[:] = other_d, theirs
        mine, theirs = yield from scan(
            state, other_state, own_flag, other_flag, sums, bits, True, gain_sums.append
        )
        final_of(0, mine)
        (got,) = yield [(theirs, 1)]
        final_of(1, got)

    doubling = levels - 3
    back = 3 + doubling
    work = {
        1: other_local_of,
        1 + doubling: local_of,
        back: first_spread_of,
        back + doubling: lambda _: (d_att[1], carried[1]),
        back + doubling + 1: last_spread_of,
    }
    run(chain(), work)
    gain_sums = jnp.stack(crossed(bits[:1] > 0.5, *gain_sums), axis=1)
    gain_grad = gain_sums.reshape(width) / math.sqrt(tokens * lax.axis_size("ctx"))
    return spread[1][0], *grads, gain_grad


def solution(mesh):
    tokens = P(("parts", "ctx"), None)
    return jax.shard_map(
        shards,
        mesh=mesh,
        in_specs=(tokens, tokens, tokens, tokens, P(), P(None, ("parts", "ctx"))),
        out_specs=(tokens, tokens, tokens, P("parts")),
        check_vma=False,
    )
```

```python
import functools
import math

import jax
import jax.numpy as jnp
from jax import lax
from jax.experimental import pallas as pl
from jax.experimental.pallas import tpu as pltpu
from jax.sharding import PartitionSpec as P

E = 128
PAIR = 2 * E
FLAG = 8
SQUARE = 4
TOGETHER = 8
EPS = 1e-06
VMEM_LIMIT = 8 * 1024 * 1024
F32 = jnp.float32
BF16 = jnp.bfloat16
VMEM = pl.BlockSpec(memory_space=pltpu.VMEM)
ANY = pl.BlockSpec(memory_space=pl.ANY)


def dot(a, b, a_dim, b_dim):
    return lax.dot_general(a, b, (((a_dim,), (b_dim,)), ((), ())), preferred_element_type=F32)


def head(h):
    return slice(h * E, (h + 1) * E)


def place(pair, pairs):
    chip = (lax.axis_index("ctx") // 2) % SQUARE
    slot = ((pair % SQUARE) ^ chip) * (pairs // SQUARE) + pair // SQUARE
    return pl.ds(pl.multiple_of(slot * E, E), E)


def owner_column(pair, other):
    core = lax.axis_index("ctx") % 2
    return pl.ds(pl.multiple_of((2 * pair + (core + other) % 2) * E, E), E)


def fetch(other, sources, targets, sems):
    copies = []
    for pair in range(targets[0].shape[1] // E):
        copies.append([])
        for i, (source, target) in enumerate(zip(sources, targets)):
            copy = pltpu.make_async_copy(
                source.at[:, owner_column(pair, other)], target.at[:, head(pair)], sems.at[pair, i]
            )
            copy.start()
            copies[-1].append(copy)
    return copies


def put(source, target, pair, other, sem):
    copy = pltpu.make_async_copy(
        source.at[:, head(pair)], target.at[:, owner_column(pair, other)], sem
    )
    copy.start()
    return copy


def row_values(values, rows, dtype):
    position = lax.broadcasted_iota(jnp.int32, (rows, E), 0)
    result = jnp.full((rows, E), values[0])
    for block in range(1, len(values)):
        result = jnp.where(position >= block * (rows // len(values)), values[block], result)
    return result.astype(dtype)


def states_of(k_ref, v_ref, tail_ref, copies, out_ref):
    pairs = len(copies)
    for begin in range(0, pairs, TOGETHER):
        together = range(begin, min(begin + TOGETHER, pairs))
        for pair in together:
            for copy in copies[pair]:
                copy.wait()
        for pair in together:
            state = dot(k_ref[:, head(pair)] * tail_ref[...], v_ref[:, head(pair)], 0, 0)
            out_ref[place(pair, pairs), :] = state


def send_state_kernel(
    bounds_hbm, k_hbm, v_hbm,
    send_ref, k_ref, v_ref, start_ref, end_ref, use_ref, tail_ref, flag_ref, bits_ref,
    bounds, sems, bounds_sem,
):
    bounds_copy = pltpu.make_async_copy(bounds_hbm, bounds, bounds_sem)
    bounds_copy.start()
    copies = fetch(1, (k_hbm, v_hbm), (k_ref, v_ref), sems)
    rows, width = k_ref.shape
    count = bounds.shape[1]
    block_len = rows // count
    me = lax.axis_index("ctx")
    first = me * count
    for bit in range(bits_ref.shape[0] // FLAG):
        value = jnp.full((FLAG, E), (me // 2**bit) % 2)
        bits_ref[bit * FLAG : (bit + 1) * FLAG, :] = value.astype(F32)
    bounds_copy.wait()
    opens = [bounds[0, b] for b in range(count)]
    closes = [bounds[1, b] for b in range(count)]
    flag = jnp.full((FLAG, E), (opens[-1] >= first).astype(F32))
    flag_ref[...] = flag
    send_ref[width:, :] = flag
    use_ref[...] = row_values([(x < first).astype(F32) for x in opens], rows, BF16)
    tail_ref[...] = row_values([(x >= first + count - 1).astype(F32) for x in closes], rows, BF16)
    start_ref[...] = row_values([(x - first) * block_len for x in opens], rows, jnp.int32)
    end_ref[...] = row_values([(x - first + 1) * block_len for x in closes], rows, jnp.int32)
    states_of(k_ref, v_ref, tail_ref, copies, send_ref)


def keep_state_kernel(k_hbm, v_hbm, tail_ref, keep_ref, k_ref, v_ref, sems):
    copies = fetch(0, (k_hbm, v_hbm), (k_ref, v_ref), sems)
    states_of(k_ref, v_ref, tail_ref, copies, keep_ref)


def sight(bound_ref, turned):
    rows = bound_ref.shape[0]
    row = lax.broadcasted_iota(jnp.int32, (rows, E), 0)
    parts = []
    for c in range(rows // E):
        column = lax.broadcasted_iota(jnp.int32, (rows, E), 1) + c * E
        if turned:
            seen = (column >= row) & (column < bound_ref[...])
        else:
            seen = (column <= row) & (column >= bound_ref[...])
        parts.append(jnp.where(seen, 1.0, 0.0).astype(BF16))
    return jnp.concatenate(parts, axis=1)


def attend(q_ref, k_ref, v_ref, copies, mask, put_out):
    pairs = len(copies)
    for begin in range(0, pairs, TOGETHER):
        together = range(begin, min(begin + TOGETHER, pairs))
        for pair in together:
            copies[pair][0].wait()
        for pair in together:
            c = head(pair)
            scores = dot(q_ref[:, c], k_ref[:, c], 1, 1).astype(BF16) * mask
            put_out(c, dot(scores, v_ref[:, c], 1, 0))


def local_kernel(
    q_hbm, g_hbm, gain_hbm, k_ref, v_ref, start_ref, _,
    out_ref, q_ref, g_ref, gain_ref, q_sems, g_sems, gain_sem,
):
    copies = fetch(0, [q_hbm], [q_ref], q_sems)
    grad_copies = fetch(0, [g_hbm], [g_ref], g_sems)
    gain_copy = pltpu.make_async_copy(gain_hbm, gain_ref, gain_sem)
    gain_copy.start()

    def put_out(c, local):
        out_ref[:, c] = local

    attend(q_ref, k_ref, v_ref, copies, sight(start_ref, False), put_out)
    for (copy,) in grad_copies:
        copy.wait()
    gain_copy.wait()


def other_local_kernel(
    q_hbm, g_hbm, k_ref, v_ref, start_ref, use_ref, _,
    out_ref, q_ref, g_ref, q_sems, g_sems,
):
    copies = fetch(1, [q_hbm], [q_ref], q_sems)
    grad_copies = fetch(1, [g_hbm], [g_ref], g_sems)
    rows = q_ref.shape[0]
    use = use_ref[...]

    def put_out(c, local):
        out_ref[:rows, c] = local
        out_ref[rows : 2 * rows, c] = (q_ref[:, c] * use).astype(F32)

    attend(q_ref, k_ref, v_ref, copies, sight(start_ref, False), put_out)
    for (copy,) in grad_copies:
        copy.wait()
    for pair in range(len(copies)):
        out_ref[2 * rows :, head(pair)] = g_ref[:, head(pair)].astype(F32)


def through_norm(local, used, grad, gain, carry):
    attended = local + dot(used, carry.astype(BF16), 1, 0)
    d_norm = grad * gain
    square = jnp.mean(attended * attended, axis=1, keepdims=True)
    centre = jnp.mean(d_norm * attended, axis=1, keepdims=True)
    inverse = lax.rsqrt(square + EPS)
    total = jnp.sum(grad * (attended * inverse), axis=0, keepdims=True)
    d_att = ((d_norm - attended * (centre * inverse * inverse)) * inverse).astype(BF16)
    return d_att, dot(used, d_att, 0, 0), total


def middle_kernel(
    q_ref, g_ref, gain_ref, local_ref, other_ref, mine_ref, theirs_ref, use_ref,
    d_ref, other_d_ref, state_ref, other_state_ref, sums_ref,
):
    rows = q_ref.shape[0]
    pairs = q_ref.shape[1] // E
    for pair in range(pairs):
        c, where = head(pair), place(pair, pairs)
        gain = gain_ref[:, owner_column(pair, 0)]
        d_att, state, total = through_norm(
            local_ref[:, c], q_ref[:, c] * use_ref[...], g_ref[:, c].astype(F32), gain,
            mine_ref[where, :],
        )
        d_ref[:, c] = d_att
        state_ref[where, :] = state
        d_att, state, other_total = through_norm(
            other_ref[:rows, c], other_ref[rows : 2 * rows, c].astype(BF16),
            other_ref[2 * rows :, c], gain, theirs_ref[where, :],
        )
        other_d_ref[:, c] = d_att.astype(F32)
        other_state_ref[where, :] = state
        sums_ref[pair : pair + 1, :] = total + other_total


def spread_kernel(
    q_ref, k_ref, v_ref, d_ref, carry_ref, use_ref, start_ref, end_ref, *rest, other
):
    qg_hbm, kp_ref, vp_ref, qg_ref, sems = rest[-5:]
    pairs = q_ref.shape[1] // E
    use = use_ref[...]
    mask = sight(start_ref, False)
    turned_mask = sight(end_ref, True)
    copies = []
    for pair in range(pairs):
        c = head(pair)
        carry = carry_ref[place(pair, pairs), :].astype(BF16)
        query, key, value, d_att = q_ref[:, c], k_ref[:, c], v_ref[:, c], d_ref[:, c].astype(BF16)
        dscores = dot(d_att, value, 1, 1).astype(BF16) * mask
        from_carry = dot(d_att * use, carry, 1, 1)
        qg_ref[:, c] = (dot(dscores, key, 1, 0) + from_carry).astype(BF16)
        turned = dot(value, d_att, 1, 1).astype(BF16) * turned_mask
        kp_ref[:, c] = dot(turned, query, 1, 0)
        turned = dot(key, query, 1, 1).astype(BF16) * turned_mask
        vp_ref[:, c] = dot(turned, d_att, 1, 0)
        copies.append(put(qg_ref, qg_hbm, pair, other, sems.at[pair]))
    for copy in copies:
        copy.wait()


def final_kernel(k_ref, v_ref, kp_ref, vp_ref, later_ref, tail_ref, *rest, other):
    kg_hbm, vg_hbm, kg_ref, vg_ref, sems = rest[-5:]
    pairs = k_ref.shape[1] // E
    tail = tail_ref[...]
    copies = []
    for pair in range(pairs):
        c = head(pair)
        later = later_ref[place(pair, pairs), :].astype(BF16)
        kg_ref[:, c] = (kp_ref[:, c] + dot(v_ref[:, c] * tail, later, 1, 1)).astype(BF16)
        vg_ref[:, c] = (vp_ref[:, c] + dot(k_ref[:, c] * tail, later, 1, 0)).astype(BF16)
        copies.append(put(kg_ref, kg_hbm, pair, other, sems.at[pair, 0]))
        copies.append(put(vg_ref, vg_hbm, pair, other, sems.at[pair, 1]))
    for copy in copies:
        copy.wait()


def swap(block, distance):
    count = lax.axis_size("ctx")
    return lax.ppermute(block, "ctx", [(i, i ^ distance) for i in range(count)])


def combine(early, late):
    return jnp.maximum(early[0], late[0]), late[1] + (1.0 - late[0]) * early[1]


def crossed(bit, zero, one):
    return jnp.where(bit, one, zero), jnp.where(bit, zero, one)


def permuted(parts, low, high):
    a, b = crossed(low, parts[0], parts[1])
    c, d = crossed(low, parts[2], parts[3])
    a, c = crossed(high, a, c)
    b, d = crossed(high, b, d)
    return [a, b, c, d]


def scan(own, partner, own_flag, partner_flag, extra, bits, backward, summed):
    count = lax.axis_size("ctx")
    rows = own.shape[0]
    part = rows // SQUARE

    def last(distance):
        row = FLAG * (distance.bit_length() - 1)
        bit = bits[row : row + 1]
        return bit < 0.5 if backward else bit > 0.5

    def packed(block, flag, extra):
        return jnp.concatenate([block, jnp.broadcast_to(flag, (FLAG, E)), extra])

    core_flag, late_flag = crossed(last(1), own_flag, partner_flag)
    first_core = jnp.where(last(1), partner, own)
    flag = jnp.maximum(core_flag, late_flag)

    def both_cores(number):
        where = slice(number * part, (number + 1) * part)
        early, late = crossed(last(1), own[where], partner[where])
        return late + (1.0 - late_flag) * early

    gots = yield [
        (packed(both_cores(number), flag, extra), 2 * number) for number in range(1, SQUARE)
    ]
    extra = sum((got[part + FLAG :] for got in gots), extra)
    flags = permuted([flag] + [got[part : part + 1] for got in gots], last(2), last(4))
    sums = permuted([both_cores(0)] + [got[:part] for got in gots], last(2), last(4))
    runs = [(flags[0], sums[0])]
    for following in list(zip(flags, sums))[1:]:
        runs.append(combine(runs[-1], following))
    flag, total = runs.pop()

    before = jnp.zeros_like(flag), jnp.zeros_like(total)
    distance = 2 * SQUARE
    while distance < count:
        (got,) = yield [(packed(total, flag, extra), distance)]
        extra = extra + got[part + FLAG :]
        got = got[part : part + 1], got[:part]
        longer = combine(got, before)
        before = [jnp.where(last(distance), new, old) for new, old in zip(longer, before)]
        after, ahead = combine((flag, total), got), combine(got, (flag, total))
        flag, total = (jnp.where(last(distance), b, a) for a, b in zip(after, ahead))
        distance *= 2

    summed(extra)
    results = [before[1]] + [combine(before, run)[1] for run in runs]
    results = permuted(results, last(2), last(4))
    gots = yield [(results[number], 2 * number) for number in range(1, SQUARE)]
    before = jnp.concatenate([results[0], *gots])
    after = first_core + (1.0 - core_flag) * before
    return crossed(last(1), before, after)


def run(chain, work):
    swaps = next(chain)
    number, done = 0, ()
    while True:
        blocks, _ = lax.optimization_barrier(([block for block, _ in swaps], done))
        done = work[number](blocks[-1]) if number in work else ()
        try:
            swaps = chain.send([swap(b, distance) for b, (_, distance) in zip(blocks, swaps)])
        except StopIteration as end:
            return end.value
        number += 1


def shards(queries, key_vectors, value_vectors, out_grad, norm_gain, doc_bounds):
    tokens, width = queries.shape
    half = width // 2
    pairs = half // E
    rows = pairs * E
    levels = lax.axis_size("ctx").bit_length() - 1
    queries, key_vectors, value_vectors, out_grad, gains, doc_bounds = (
        pltpu.with_memory_space_constraint(x, pltpu.HBM)
        for x in (
            queries, key_vectors, value_vectors, out_grad, norm_gain.reshape(1, width), doc_bounds
        )
    )

    def held(count, columns, dtype=F32, spec=VMEM):
        return spec, jax.ShapeDtypeStruct((count, columns), dtype)

    def call(kernel, inputs, outputs, scratch=(), aliases={}, **sizes):
        return pl.pallas_call(
            functools.partial(kernel, **sizes),
            in_specs=inputs,
            out_specs=[spec for spec, _ in outputs],
            out_shape=[out for _, out in outputs],
            scratch_shapes=scratch,
            input_output_aliases=aliases,
            compiler_params=pltpu.CompilerParams(vmem_limit_bytes=VMEM_LIMIT),
        )

    def copies(*counts):
        return pltpu.SemaphoreType.DMA(counts)

    narrow, single = held(tokens, half, BF16), held(tokens, half)
    grad = held(tokens, width, BF16, ANY)
    row = held(tokens, E, BF16)
    staging = pltpu.VMEM((tokens, half), BF16)
    keys, values, query, local, carried, d_att, spread = {}, {}, {}, {}, {}, {}, {}
    norm_inputs, middle = [], []
    send, keys[1], values[1], start, end, use, tail, flag, bits = call(
        send_state_kernel,
        [ANY] * 3,
        [held(rows + FLAG, E), narrow, narrow, held(tokens, E, jnp.int32),
         held(tokens, E, jnp.int32), row, row, held(FLAG, E), held(FLAG * levels, E)],
        [pltpu.SMEM(doc_bounds.shape, jnp.int32), copies(pairs, 2), copies()],
    )(doc_bounds, key_vectors, value_vectors)
    keep, keys[0], values[0] = call(
        keep_state_kernel,
        [ANY, ANY, VMEM],
        [held(rows, E), narrow, narrow],
        [copies(pairs, 2)],
    )(key_vectors, value_vectors, tail)

    def other_local_of(token):
        pack, other_query = call(
            other_local_kernel,
            [ANY] * 2 + [VMEM] * 4 + [ANY],
            [held(3 * tokens, half), narrow],
            [pltpu.VMEM((tokens, half), BF16), copies(pairs, 1), copies(pairs, 1)],
        )(queries, out_grad, keys[1], values[1], start, use, token)
        query[1] = other_query
        middle[:] = [pack]
        return other_query

    def exchange(block):
        local[1] = swap(lax.optimization_barrier((middle[0], block))[0], 1)
        return ()

    def local_of(token):
        local[0], query[0], *rest = call(
            local_kernel,
            [ANY] * 3 + [VMEM] * 3 + [ANY],
            [single, narrow, narrow, held(1, width)],
            [copies(pairs, 1), copies(pairs, 1), copies()],
        )(queries, out_grad, gains, keys[0], values[0], start, token)
        norm_inputs[:] = rest
        return local[0]

    def spread_of(other, token):
        done = spread[0][:1] if other else []
        spread[other] = call(
            spread_kernel,
            [VMEM] * 8 + [ANY] * (1 + len(done)),
            [grad, single, single],
            [staging, copies(pairs)],
            {9: 0} if done else {},
            other=other,
        )(
            query[other], keys[other], values[other], d_att[other], carried[other],
            use, start, end, token, *done,
        )
        return spread[other][1]

    def first_spread_of(token):
        done = spread_of(0, token)
        d_other, theirs = lax.optimization_barrier((middle, done))[0]
        d_att[1], carried[1] = swap(d_other, 1), swap(theirs, 1)
        return done

    def last_spread_of(token):
        done = spread_of(1, token)
        sums = lax.optimization_barrier((gain_sums[0], done))[0]
        gain_sums.append(swap(sums, 1))
        return done, gain_sums[1]

    grads, gain_sums = [], []

    def final_of(other, later):
        grads[:] = call(
            final_kernel,
            [VMEM] * 6 + [ANY] * len(grads),
            [grad, grad],
            [staging, staging, copies(pairs, 2)],
            {6: 0, 7: 1} if grads else {},
            other=other,
        )(keys[other], values[other], *spread[other][1:], later, tail, *grads)

    def chain():
        (got,) = yield [(send, 1)]
        own_flag, other_flag = flag[:1], got[rows : rows + 1]
        nothing = jnp.zeros((0, E), F32)
        mine, theirs = yield from scan(
            keep, got[:rows], own_flag, other_flag, nothing, bits, False, lambda _: None
        )
        carried[0] = mine
        d_att[0], other_d, state, other_state, sums = call(
            middle_kernel,
            [VMEM] * 8,
            [narrow, single, held(rows, E), held(rows, E), held(pairs, E)],
        )(query[0], *norm_inputs, local[0], local[1], mine, theirs, use)
        middle[:] = other_d, theirs
        mine, theirs = yield from scan(
            state, other_state, own_flag, other_flag, sums, bits, True, gain_sums.append
        )
        final_of(0, mine)
        (got,) = yield [(theirs, 1)]
        final_of(1, got)

    doubling = levels - 3
    back = 3 + doubling
    work = {
        1: other_local_of,
        1 + doubling: local_of,
        2 + doubling: exchange,
        back: first_spread_of,
        back + doubling: lambda _: (d_att[1], carried[1]),
        back + doubling + 1: last_spread_of,
    }
    run(chain(), work)
    gain_sums = jnp.stack(crossed(bits[:1] > 0.5, *gain_sums), axis=1)
    gain_grad = gain_sums.reshape(width) / math.sqrt(tokens * lax.axis_size("ctx"))
    return spread[1][0], *grads, gain_grad


def solution(mesh):
    tokens = P(("parts", "ctx"), None)
    return jax.shard_map(
        shards,
        mesh=mesh,
        in_specs=(tokens, tokens, tokens, tokens, P(), P(None, ("parts", "ctx"))),
        out_specs=(tokens, tokens, tokens, P("parts")),
        check_vma=False,
    )
```

```python
import functools
import math

import jax
import jax.numpy as jnp
from jax import lax
from jax.experimental import pallas as pl
from jax.experimental.pallas import tpu as pltpu
from jax.sharding import PartitionSpec as P

E = 128
PAIR = 2 * E
FLAG = 8
SQUARE = 4
TOGETHER = 8
EPS = 1e-06
VMEM_LIMIT = 8 * 1024 * 1024
F32 = jnp.float32
BF16 = jnp.bfloat16
VMEM = pl.BlockSpec(memory_space=pltpu.VMEM)
ANY = pl.BlockSpec(memory_space=pl.ANY)


def dot(a, b, a_dim, b_dim):
    return lax.dot_general(a, b, (((a_dim,), (b_dim,)), ((), ())), preferred_element_type=F32)


def head(h):
    return slice(h * E, (h + 1) * E)


def place(pair, pairs):
    chip = (lax.axis_index("ctx") // 2) % SQUARE
    slot = ((pair % SQUARE) ^ chip) * (pairs // SQUARE) + pair // SQUARE
    return pl.ds(pl.multiple_of(slot * E, E), E)


def owner_column(pair, other):
    core = lax.axis_index("ctx") % 2
    return pl.ds(pl.multiple_of((2 * pair + (core + other) % 2) * E, E), E)


def fetch(other, sources, targets, sems):
    copies = []
    for pair in range(targets[0].shape[1] // E):
        copies.append([])
        for i, (source, target) in enumerate(zip(sources, targets)):
            copy = pltpu.make_async_copy(
                source.at[:, owner_column(pair, other)], target.at[:, head(pair)], sems.at[pair, i]
            )
            copy.start()
            copies[-1].append(copy)
    return copies


def put(source, target, pair, other, sem):
    copy = pltpu.make_async_copy(
        source.at[:, head(pair)], target.at[:, owner_column(pair, other)], sem
    )
    copy.start()
    return copy


def row_values(values, rows, dtype):
    position = lax.broadcasted_iota(jnp.int32, (rows, E), 0)
    result = jnp.full((rows, E), values[0])
    for block in range(1, len(values)):
        result = jnp.where(position >= block * (rows // len(values)), values[block], result)
    return result.astype(dtype)


def states_of(k_ref, v_ref, tail_ref, copies, out_ref):
    pairs = len(copies)
    for begin in range(0, pairs, TOGETHER):
        together = range(begin, min(begin + TOGETHER, pairs))
        for pair in together:
            for copy in copies[pair]:
                copy.wait()
        for pair in together:
            state = dot(k_ref[:, head(pair)] * tail_ref[...], v_ref[:, head(pair)], 0, 0)
            out_ref[place(pair, pairs), :] = state


def send_state_kernel(
    bounds_hbm, k_hbm, v_hbm,
    send_ref, k_ref, v_ref, start_ref, end_ref, use_ref, tail_ref, flag_ref, bits_ref,
    bounds, sems, bounds_sem,
):
    bounds_copy = pltpu.make_async_copy(bounds_hbm, bounds, bounds_sem)
    bounds_copy.start()
    copies = fetch(1, (k_hbm, v_hbm), (k_ref, v_ref), sems)
    rows, width = k_ref.shape
    count = bounds.shape[1]
    block_len = rows // count
    me = lax.axis_index("ctx")
    first = me * count
    for bit in range(bits_ref.shape[0] // FLAG):
        value = jnp.full((FLAG, E), (me // 2**bit) % 2)
        bits_ref[bit * FLAG : (bit + 1) * FLAG, :] = value.astype(F32)
    bounds_copy.wait()
    opens = [bounds[0, b] for b in range(count)]
    closes = [bounds[1, b] for b in range(count)]
    flag = jnp.full((FLAG, E), (opens[-1] >= first).astype(F32))
    flag_ref[...] = flag
    send_ref[width:, :] = flag
    use_ref[...] = row_values([(x < first).astype(F32) for x in opens], rows, BF16)
    tail_ref[...] = row_values([(x >= first + count - 1).astype(F32) for x in closes], rows, BF16)
    start_ref[...] = row_values([(x - first) * block_len for x in opens], rows, jnp.int32)
    end_ref[...] = row_values([(x - first + 1) * block_len for x in closes], rows, jnp.int32)
    states_of(k_ref, v_ref, tail_ref, copies, send_ref)


def keep_state_kernel(k_hbm, v_hbm, tail_ref, keep_ref, k_ref, v_ref, sems):
    copies = fetch(0, (k_hbm, v_hbm), (k_ref, v_ref), sems)
    states_of(k_ref, v_ref, tail_ref, copies, keep_ref)


def sight(bound_ref, turned):
    rows = bound_ref.shape[0]
    row = lax.broadcasted_iota(jnp.int32, (rows, E), 0)
    parts = []
    for c in range(rows // E):
        column = lax.broadcasted_iota(jnp.int32, (rows, E), 1) + c * E
        if turned:
            seen = (column >= row) & (column < bound_ref[...])
        else:
            seen = (column <= row) & (column >= bound_ref[...])
        parts.append(jnp.where(seen, 1.0, 0.0).astype(BF16))
    return jnp.concatenate(parts, axis=1)


def attend(q_ref, k_ref, v_ref, copies, mask, put_out):
    pairs = len(copies)
    for begin in range(0, pairs, TOGETHER):
        together = range(begin, min(begin + TOGETHER, pairs))
        for pair in together:
            copies[pair][0].wait()
        for pair in together:
            c = head(pair)
            scores = dot(q_ref[:, c], k_ref[:, c], 1, 1).astype(BF16) * mask
            put_out(c, dot(scores, v_ref[:, c], 1, 0))


def local_kernel(
    q_hbm, g_hbm, gain_hbm, k_ref, v_ref, start_ref, _,
    out_ref, q_ref, g_ref, gain_ref, q_sems, g_sems, gain_sem,
):
    copies = fetch(0, [q_hbm], [q_ref], q_sems)
    grad_copies = fetch(0, [g_hbm], [g_ref], g_sems)
    gain_copy = pltpu.make_async_copy(gain_hbm, gain_ref, gain_sem)
    gain_copy.start()

    def put_out(c, local):
        out_ref[:, c] = local

    attend(q_ref, k_ref, v_ref, copies, sight(start_ref, False), put_out)
    for (copy,) in grad_copies:
        copy.wait()
    gain_copy.wait()


def other_local_kernel(
    q_hbm, g_hbm, k_ref, v_ref, start_ref, use_ref, _,
    out_ref, q_ref, g_ref, q_sems, g_sems,
):
    copies = fetch(1, [q_hbm], [q_ref], q_sems)
    grad_copies = fetch(1, [g_hbm], [g_ref], g_sems)
    rows = q_ref.shape[0]
    use = use_ref[...]

    def put_out(c, local):
        out_ref[:rows, c] = local
        out_ref[rows : 2 * rows, c] = (q_ref[:, c] * use).astype(F32)

    attend(q_ref, k_ref, v_ref, copies, sight(start_ref, False), put_out)
    for (copy,) in grad_copies:
        copy.wait()
    for pair in range(len(copies)):
        out_ref[2 * rows :, head(pair)] = g_ref[:, head(pair)].astype(F32)


def through_norm(local, used, grad, gain, carry):
    attended = local + dot(used, carry.astype(BF16), 1, 0)
    d_norm = grad * gain
    square = jnp.sum(attended * attended, axis=1, keepdims=True)
    along = jnp.sum(d_norm * attended, axis=1, keepdims=True)
    inverse = lax.rsqrt(square * (1.0 / E) + EPS)
    normed = attended * inverse
    total = jnp.sum(grad * normed, axis=0, keepdims=True)
    d_att = ((d_norm - normed * (along * inverse * (1.0 / E))) * inverse).astype(BF16)
    return d_att, dot(used, d_att, 0, 0), total


def middle_kernel(
    q_ref, g_ref, gain_ref, local_ref, other_ref, mine_ref, theirs_ref, use_ref,
    d_ref, other_d_ref, state_ref, other_state_ref, sums_ref,
):
    rows = q_ref.shape[0]
    pairs = q_ref.shape[1] // E
    for pair in range(pairs):
        c, where = head(pair), place(pair, pairs)
        gain = gain_ref[:, owner_column(pair, 0)]
        d_att, state, total = through_norm(
            local_ref[:, c], q_ref[:, c] * use_ref[...], g_ref[:, c].astype(F32), gain,
            mine_ref[where, :],
        )
        d_ref[:, c] = d_att
        state_ref[where, :] = state
        d_att, state, other_total = through_norm(
            other_ref[:rows, c], other_ref[rows : 2 * rows, c].astype(BF16),
            other_ref[2 * rows :, c], gain, theirs_ref[where, :],
        )
        other_d_ref[:, c] = d_att.astype(F32)
        other_state_ref[where, :] = state
        sums_ref[pair : pair + 1, :] = total + other_total


def spread_kernel(
    q_ref, k_ref, v_ref, d_ref, carry_ref, use_ref, start_ref, end_ref, *rest, other
):
    qg_hbm, kp_ref, vp_ref, qg_ref, sems = rest[-5:]
    pairs = q_ref.shape[1] // E
    use = use_ref[...]
    mask = sight(start_ref, False)
    turned_mask = sight(end_ref, True)
    copies = []
    for pair in range(pairs):
        c = head(pair)
        carry = carry_ref[place(pair, pairs), :].astype(BF16)
        query, key, value, d_att = q_ref[:, c], k_ref[:, c], v_ref[:, c], d_ref[:, c].astype(BF16)
        dscores = dot(d_att, value, 1, 1).astype(BF16) * mask
        from_carry = dot(d_att * use, carry, 1, 1)
        qg_ref[:, c] = (dot(dscores, key, 1, 0) + from_carry).astype(BF16)
        turned = dot(value, d_att, 1, 1).astype(BF16) * turned_mask
        kp_ref[:, c] = dot(turned, query, 1, 0)
        turned = dot(key, query, 1, 1).astype(BF16) * turned_mask
        vp_ref[:, c] = dot(turned, d_att, 1, 0)
        copies.append(put(qg_ref, qg_hbm, pair, other, sems.at[pair]))
    for copy in copies:
        copy.wait()


def final_kernel(k_ref, v_ref, kp_ref, vp_ref, later_ref, tail_ref, *rest, other):
    kg_hbm, vg_hbm, kg_ref, vg_ref, sems = rest[-5:]
    pairs = k_ref.shape[1] // E
    tail = tail_ref[...]
    copies = []
    for pair in range(pairs):
        c = head(pair)
        later = later_ref[place(pair, pairs), :].astype(BF16)
        kg_ref[:, c] = (kp_ref[:, c] + dot(v_ref[:, c] * tail, later, 1, 1)).astype(BF16)
        vg_ref[:, c] = (vp_ref[:, c] + dot(k_ref[:, c] * tail, later, 1, 0)).astype(BF16)
        copies.append(put(kg_ref, kg_hbm, pair, other, sems.at[pair, 0]))
        copies.append(put(vg_ref, vg_hbm, pair, other, sems.at[pair, 1]))
    for copy in copies:
        copy.wait()


def swap(block, distance):
    count = lax.axis_size("ctx")
    return lax.ppermute(block, "ctx", [(i, i ^ distance) for i in range(count)])


def combine(early, late):
    return jnp.maximum(early[0], late[0]), late[1] + (1.0 - late[0]) * early[1]


def crossed(bit, zero, one):
    return jnp.where(bit, one, zero), jnp.where(bit, zero, one)


def permuted(parts, low, high):
    a, b = crossed(low, parts[0], parts[1])
    c, d = crossed(low, parts[2], parts[3])
    a, c = crossed(high, a, c)
    b, d = crossed(high, b, d)
    return [a, b, c, d]


def scan(own, partner, own_flag, partner_flag, extra, bits, backward, summed):
    count = lax.axis_size("ctx")
    rows = own.shape[0]
    part = rows // SQUARE

    def last(distance):
        row = FLAG * (distance.bit_length() - 1)
        bit = bits[row : row + 1]
        return bit < 0.5 if backward else bit > 0.5

    def packed(block, flag, extra):
        return jnp.concatenate([block, jnp.broadcast_to(flag, (FLAG, E)), extra])

    core_flag, late_flag = crossed(last(1), own_flag, partner_flag)
    first_core = jnp.where(last(1), partner, own)
    flag = jnp.maximum(core_flag, late_flag)

    def both_cores(number):
        where = slice(number * part, (number + 1) * part)
        early, late = crossed(last(1), own[where], partner[where])
        return late + (1.0 - late_flag) * early

    gots = yield [
        (packed(both_cores(number), flag, extra), 2 * number) for number in range(1, SQUARE)
    ]
    extra = sum((got[part + FLAG :] for got in gots), extra)
    flags = permuted([flag] + [got[part : part + 1] for got in gots], last(2), last(4))
    sums = permuted([both_cores(0)] + [got[:part] for got in gots], last(2), last(4))
    runs = [(flags[0], sums[0])]
    for following in list(zip(flags, sums))[1:]:
        runs.append(combine(runs[-1], following))
    flag, total = runs.pop()

    before = jnp.zeros_like(flag), jnp.zeros_like(total)
    distance = 2 * SQUARE
    while distance < count:
        (got,) = yield [(packed(total, flag, extra), distance)]
        extra = extra + got[part + FLAG :]
        got = got[part : part + 1], got[:part]
        longer = combine(got, before)
        before = [jnp.where(last(distance), new, old) for new, old in zip(longer, before)]
        after, ahead = combine((flag, total), got), combine(got, (flag, total))
        flag, total = (jnp.where(last(distance), b, a) for a, b in zip(after, ahead))
        distance *= 2

    summed(extra)
    results = [before[1]] + [combine(before, run)[1] for run in runs]
    results = permuted(results, last(2), last(4))
    gots = yield [(results[number], 2 * number) for number in range(1, SQUARE)]
    before = jnp.concatenate([results[0], *gots])
    after = first_core + (1.0 - core_flag) * before
    return crossed(last(1), before, after)


def run(chain, work):
    swaps = next(chain)
    number, done = 0, ()
    while True:
        blocks, _ = lax.optimization_barrier(([block for block, _ in swaps], done))
        done = work[number](blocks[-1]) if number in work else ()
        try:
            swaps = chain.send([swap(b, distance) for b, (_, distance) in zip(blocks, swaps)])
        except StopIteration as end:
            return end.value
        number += 1


def shards(queries, key_vectors, value_vectors, out_grad, norm_gain, doc_bounds):
    tokens, width = queries.shape
    half = width // 2
    pairs = half // E
    rows = pairs * E
    levels = lax.axis_size("ctx").bit_length() - 1
    queries, key_vectors, value_vectors, out_grad, gains, doc_bounds = (
        pltpu.with_memory_space_constraint(x, pltpu.HBM)
        for x in (
            queries, key_vectors, value_vectors, out_grad, norm_gain.reshape(1, width), doc_bounds
        )
    )

    def held(count, columns, dtype=F32, spec=VMEM):
        return spec, jax.ShapeDtypeStruct((count, columns), dtype)

    def call(kernel, inputs, outputs, scratch=(), aliases={}, **sizes):
        return pl.pallas_call(
            functools.partial(kernel, **sizes),
            in_specs=inputs,
            out_specs=[spec for spec, _ in outputs],
            out_shape=[out for _, out in outputs],
            scratch_shapes=scratch,
            input_output_aliases=aliases,
            compiler_params=pltpu.CompilerParams(vmem_limit_bytes=VMEM_LIMIT),
        )

    def copies(*counts):
        return pltpu.SemaphoreType.DMA(counts)

    narrow, single = held(tokens, half, BF16), held(tokens, half)
    grad = held(tokens, width, BF16, ANY)
    row = held(tokens, E, BF16)
    staging = pltpu.VMEM((tokens, half), BF16)
    keys, values, query, local, carried, d_att, spread = {}, {}, {}, {}, {}, {}, {}
    norm_inputs, middle = [], []
    send, keys[1], values[1], start, end, use, tail, flag, bits = call(
        send_state_kernel,
        [ANY] * 3,
        [held(rows + FLAG, E), narrow, narrow, held(tokens, E, jnp.int32),
         held(tokens, E, jnp.int32), row, row, held(FLAG, E), held(FLAG * levels, E)],
        [pltpu.SMEM(doc_bounds.shape, jnp.int32), copies(pairs, 2), copies()],
    )(doc_bounds, key_vectors, value_vectors)
    keep, keys[0], values[0] = call(
        keep_state_kernel,
        [ANY, ANY, VMEM],
        [held(rows, E), narrow, narrow],
        [copies(pairs, 2)],
    )(key_vectors, value_vectors, tail)

    def other_local_of(token):
        pack, other_query = call(
            other_local_kernel,
            [ANY] * 2 + [VMEM] * 4 + [ANY],
            [held(3 * tokens, half), narrow],
            [pltpu.VMEM((tokens, half), BF16), copies(pairs, 1), copies(pairs, 1)],
        )(queries, out_grad, keys[1], values[1], start, use, token)
        query[1] = other_query
        middle[:] = [pack]
        return other_query

    def exchange(block):
        local[1] = swap(lax.optimization_barrier((middle[0], block))[0], 1)
        return ()

    def local_of(token):
        local[0], query[0], *rest = call(
            local_kernel,
            [ANY] * 3 + [VMEM] * 3 + [ANY],
            [single, narrow, narrow, held(1, width)],
            [copies(pairs, 1), copies(pairs, 1), copies()],
        )(queries, out_grad, gains, keys[0], values[0], start, token)
        norm_inputs[:] = rest
        return local[0]

    def spread_of(other, token):
        done = spread[0][:1] if other else []
        spread[other] = call(
            spread_kernel,
            [VMEM] * 8 + [ANY] * (1 + len(done)),
            [grad, single, single],
            [staging, copies(pairs)],
            {9: 0} if done else {},
            other=other,
        )(
            query[other], keys[other], values[other], d_att[other], carried[other],
            use, start, end, token, *done,
        )
        return spread[other][1]

    def first_spread_of(token):
        done = spread_of(0, token)
        d_other, theirs = lax.optimization_barrier((middle, done))[0]
        d_att[1], carried[1] = swap(d_other, 1), swap(theirs, 1)
        return done

    def last_spread_of(token):
        done = spread_of(1, token)
        sums = lax.optimization_barrier((gain_sums[0], done))[0]
        gain_sums.append(swap(sums, 1))
        return done, gain_sums[1]

    grads, gain_sums = [], []

    def final_of(other, later):
        grads[:] = call(
            final_kernel,
            [VMEM] * 6 + [ANY] * len(grads),
            [grad, grad],
            [staging, staging, copies(pairs, 2)],
            {6: 0, 7: 1} if grads else {},
            other=other,
        )(keys[other], values[other], *spread[other][1:], later, tail, *grads)

    def chain():
        (got,) = yield [(send, 1)]
        own_flag, other_flag = flag[:1], got[rows : rows + 1]
        nothing = jnp.zeros((0, E), F32)
        mine, theirs = yield from scan(
            keep, got[:rows], own_flag, other_flag, nothing, bits, False, lambda _: None
        )
        carried[0] = mine
        d_att[0], other_d, state, other_state, sums = call(
            middle_kernel,
            [VMEM] * 8,
            [narrow, single, held(rows, E), held(rows, E), held(pairs, E)],
        )(query[0], *norm_inputs, local[0], local[1], mine, theirs, use)
        middle[:] = other_d, theirs
        mine, theirs = yield from scan(
            state, other_state, own_flag, other_flag, sums, bits, True, gain_sums.append
        )
        final_of(0, mine)
        (got,) = yield [(theirs, 1)]
        final_of(1, got)

    doubling = levels - 3
    back = 3 + doubling
    work = {
        1: other_local_of,
        1 + doubling: local_of,
        2 + doubling: exchange,
        back: first_spread_of,
        back + doubling: lambda _: (d_att[1], carried[1]),
        back + doubling + 1: last_spread_of,
    }
    run(chain(), work)
    gain_sums = jnp.stack(crossed(bits[:1] > 0.5, *gain_sums), axis=1)
    gain_grad = gain_sums.reshape(width) / math.sqrt(tokens * lax.axis_size("ctx"))
    return spread[1][0], *grads, gain_grad


def solution(mesh):
    tokens = P(("parts", "ctx"), None)
    return jax.shard_map(
        shards,
        mesh=mesh,
        in_specs=(tokens, tokens, tokens, tokens, P(), P(None, ("parts", "ctx"))),
        out_specs=(tokens, tokens, tokens, P("parts")),
        check_vma=False,
    )
```
